512 devices in a mesh: map: 16 (over z), gx: 4 (over x_hi, core), gy: 8 (over x_lo, y).
Axes of the slice: x: 4 (x_hi: 2, x_lo: 2; x = x_hi * 2 + x_lo), y: 4, z: 16, core: 2. Of those that a mesh axis runs over, the one named last changes fastest.
Arguments:
- densities: float32 [16, 1536, 8192], P('map', 'gx', 'gy'), may hold values from 0.2 to 41, as said below
- scaling: float32 [16, 1536, 8192], P('map', 'gx', 'gy'), may hold values from 0.5 to 2
- weights: float32 [16], P('map'), as said below
Outputs:
- barycenter: float32 [1536, 8192], P('gx', 'gy')
- new_scaling: float32 [16, 1536, 8192], P('map', 'gx', 'gy')
The draws below stay inside these ranges and needn't reach their ends.
Inputs may be any that keep to these rules, and one draw needn't show every extreme that they name: `densities`: every cell's demand density is positive. The weights are positive and sum to one.
All inputs are finite; a program needn't handle non-finite values.
Results may differ from the reference program's by a relative error of at most 0.0001.
Values sent between devices are 32-bit elements; how exact they have to be, the bound alone decides.
A program may use at most 64 MiB of HBM per device.

```python
import math
import jax
import jax.numpy as jnp
from jax import lax

HALF = 32
SIGMA = 16
NX = 1536
NY = 8192
MAPS = 16


def draw_densities(key, part):
    key_hour = jax.random.fold_in(key, 11)
    key_cell = jax.random.fold_in(key, 23)
    rows = jnp.arange(NX, dtype=jnp.float32) / jnp.float32(NX - 1)
    cols = jnp.arange(NY, dtype=jnp.float32) / jnp.float32(NY - 1)
    trend = (1.0 + 2.0 * rows)[:, None] * (1.0 + 2.0 * cols)[None, :]
    hour = jnp.exp(jax.random.uniform(key_hour, (MAPS, 1, 1), jnp.float32, -0.69, 0.69))
    rough = jnp.exp(jax.random.uniform(key_cell, (MAPS, NX, NY), jnp.float32, -0.8, 0.8))
    return (trend[None, :, :] * hour * rough).astype(jnp.float32)


def draw_weights(key, part):
    key_weight = jax.random.fold_in(key, 37)
    raw = jnp.exp(jax.random.uniform(key_weight, (MAPS,), jnp.float32, -0.69, 0.69))
    return (raw / jnp.sum(raw)).astype(jnp.float32)


def level_of(key, dims, shards, low, largest):
    level = 1.0
    for position, parts in shards:
        draws = jax.random.uniform(jax.random.fold_in(jax.random.fold_in(key, 6), position), (parts,), jnp.float32, low / len(shards), largest / len(shards))
        level = level * jnp.repeat(jnp.exp(draws), dims[position] // parts).reshape((-1,) + (1,) * (len(dims) - 1 - position))
    return level


def setup_inputs(seed: int = 0) -> dict:
    key_of = jax.random.split(jax.random.key(seed), 4)
    return {
        "densities": draw_densities(jax.random.fold_in(key_of[3], 71), 0),
        "scaling": jnp.clip(jnp.exp(math.log(2.0) - 1.3862944 * jax.random.uniform(key_of[1], (MAPS, NX, NY), jnp.float32) ** level_of(key_of[1], (MAPS, NX, NY), ((0, 16), (1, 4), (2, 8)), -0.2, 0.2)), 0.5, 2.0),
        "weights": draw_weights(jax.random.fold_in(key_of[3], 71), 0),
    }


def kernel_band(count):
    rows = jnp.arange(count, dtype=jnp.int32)[:, None]
    cols = jnp.arange(count + 2 * HALF, dtype=jnp.int32)[None, :]
    offset = (cols - rows - HALF).astype(jnp.float32)
    inside = jnp.abs(cols - rows - HALF) <= HALF
    taps = jnp.arange(2 * HALF + 1, dtype=jnp.float32) - HALF
    total = jnp.sum(jnp.exp(-taps * taps / (2.0 * SIGMA * SIGMA)))
    values = jnp.exp(-offset * offset / (2.0 * SIGMA * SIGMA)) / total
    return jnp.where(inside, values, jnp.float32(0.0))


def smooth_axis(padded, axis, length):
    block = min(128, length)
    nblocks = length // block
    pieces = -(-(block + 2 * HALF) // block)
    extra = (nblocks + pieces - 1) * block - (length + 2 * HALF)
    widths = [(0, 0)] * padded.ndim
    widths[axis] = (0, extra)
    padded = jnp.pad(padded, widths)
    band = kernel_band(block)
    band = jnp.pad(band, ((0, 0), (0, pieces * block - block - 2 * HALF)))
    result = None
    for index in range(pieces):
        piece = lax.slice_in_dim(padded, index * block, index * block + length, axis=axis)
        small = band[:, index * block:(index + 1) * block]
        if axis == 1:
            piece = piece.reshape(piece.shape[0], nblocks, block, piece.shape[2])
            term = jnp.einsum("ic,mbcj->mbij", small, piece, precision=lax.Precision.HIGHEST, preferred_element_type=jnp.float32)
        else:
            piece = piece.reshape(piece.shape[0], piece.shape[1], nblocks, block)
            term = jnp.einsum("mibc,kc->mibk", piece, small, precision=lax.Precision.HIGHEST, preferred_element_type=jnp.float32)
        result = term if result is None else result + term
    if axis == 1:
        return result.reshape(result.shape[0], length, result.shape[3])
    return result.reshape(result.shape[0], result.shape[1], length)


def convolve(field):
    stack = field[None, :, :]
    tall = jnp.pad(stack, ((0, 0), (HALF, HALF), (0, 0)))
    rows_done = smooth_axis(tall, 1, field.shape[0])
    broad = jnp.pad(rows_done, ((0, 0), (0, 0), (HALF, HALF)))
    return smooth_axis(broad, 2, field.shape[1])[0]


def reference(densities, scaling, weights):
    def per_map(items):
        density, scale, weight = items
        kv = convolve(scale)
        u_field = density / kv
        ku = convolve(u_field)
        return ku, weight * jnp.log(scale * ku)

    ku, terms = lax.map(per_map, (densities, scaling, weights))
    logsum = jnp.sum(terms, axis=0)
    raw = jnp.exp(logsum)
    mass = jnp.sum(raw)
    barycenter = jnp.float32(NX * NY) * raw / mass
    new_scaling = barycenter[None, :, :] / ku
    return barycenter, new_scaling
```

```python
import functools

import jax
import jax.numpy as jnp
import ml_dtypes
import numpy as np
from jax import lax
from jax.experimental import pallas as pl
from jax.experimental.pallas import tpu as pltpu
from jax.sharding import PartitionSpec as P

HALF = 32
SIGMA = 16
LANES = 128
BLOCK = 256
SUBS = 2
MESH = pl.DeviceIdType.MESH


def band(count_out, count_in, shift):
    taps = np.arange(-HALF, HALF + 1, dtype=np.float64)
    total = np.sum(np.exp(-taps * taps / (2.0 * SIGMA * SIGMA)))
    offset = np.arange(count_in)[None, :] - np.arange(count_out)[:, None] - shift
    values = np.exp(-(offset.astype(np.float64) ** 2) / (2.0 * SIGMA * SIGMA)) / total
    values = np.where(np.abs(offset) <= HALF, values, 0.0)
    high = values.astype(ml_dtypes.bfloat16)
    low = (values - high.astype(np.float64)).astype(ml_dtypes.bfloat16)
    return np.stack([high, low])


def split(x):
    high = x.astype(jnp.bfloat16)
    low = (x - high.astype(jnp.float32)).astype(jnp.bfloat16)
    return high, low


def dot(a, b):
    return jnp.dot(a, b, preferred_element_type=jnp.float32)


def dot3(a_high, a_low, b_high, b_low):
    return dot(a_high, b_high) + (dot(a_high, b_low) + dot(a_low, b_high))


def kernel(
    sizes,
    rows,
    cols,
    s_hbm,
    d_hbm,
    w_ref,
    brow1,
    brow2,
    bcol,
    raw_ref,
    ku_ref,
    norm_ref,
    s_ext,
    d_ext,
    y_high,
    y_low,
    u_high,
    u_low,
    term,
    pack,
    strip,
    cw,
    ccw,
    m_out,
    m_gx,
    m_gy,
    m_map,
    in_sem,
    halo_send,
    halo_recv,
    cw_send,
    cw_recv,
    ccw_send,
    ccw_recv,
    acw_send,
    acw_recv,
    accw_send,
    accw_recv,
    m_gx_sem,
    m_gy_sem,
    m_map_sem,
):
    n, ngx, ngy = sizes
    z, gx, gy = lax.axis_index("map"), lax.axis_index("gx"), lax.axis_index("gy")
    wide = 2 * HALF
    left, right = LANES, LANES + cols
    s_top, s_bottom = wide, wide + rows
    d_top, d_bottom = HALF, HALF + rows

    load_s = pltpu.make_async_copy(
        s_hbm.at[0], s_ext.at[pl.ds(s_top, rows), pl.ds(left, cols)], in_sem.at[0]
    )
    load_d = pltpu.make_async_copy(
        d_hbm.at[0], d_ext.at[pl.ds(d_top, rows), pl.ds(left, cols)], in_sem.at[1]
    )
    load_s.start()
    load_d.start()

    near = []
    for dx in (-1, 0, 1):
        for dy in (-1, 0, 1):
            if dx or dy:
                ok = (gx + dx >= 0) & (gx + dx < ngx) & (gy + dy >= 0) & (gy + dy < ngy)
                near.append((dx, dy, ok))

    barrier = pltpu.get_barrier_semaphore()
    expected = jnp.int32(0)
    for dx, dy, ok in near:
        expected = expected + ok.astype(jnp.int32)

        @pl.when(ok)
        def _():
            pl.semaphore_signal(
                barrier, inc=1, device_id={"gx": gx + dx, "gy": gy + dy}, device_id_type=MESH
            )

    for axis, me, count in (("gx", gx, ngx), ("gy", gy, ngy), ("map", z, n)):
        for k in range(1, count):
            pl.semaphore_signal(
                barrier,
                inc=1,
                device_id={axis: lax.rem(me + k, count)},
                device_id_type=MESH,
            )
        expected = expected + (count - 1)
    pl.semaphore_wait(barrier, expected)

    def side(delta):
        return 0 if delta > 0 else 1

    def row_copies(dx):
        first = 0 if dx < 0 else rows - wide
        s_at = s_bottom if dx < 0 else 0
        d_first = 0 if dx < 0 else rows - HALF
        d_at = d_bottom if dx < 0 else 0
        slot = side(dx)
        to = {"gx": gx + dx}
        return (
            pltpu.make_async_remote_copy(
                s_hbm.at[0, pl.ds(first, wide)],
                s_ext.at[pl.ds(s_at, wide), pl.ds(left, cols)],
                halo_send.at[slot],
                halo_recv.at[slot],
                device_id=to,
                device_id_type=MESH,
            ),
            pltpu.make_async_remote_copy(
                d_hbm.at[0, pl.ds(d_first, HALF)],
                d_ext.at[pl.ds(d_at, HALF), pl.ds(left, cols)],
                halo_send.at[2 + slot],
                halo_recv.at[2 + slot],
                device_id=to,
                device_id_type=MESH,
            ),
        )

    def col_copy(dx, dy):
        if dx == 0:
            src, at, size, slot = 0, s_top, rows, 4 + side(dy)
        else:
            src = 0 if dx < 0 else rows - wide
            at, size = (s_bottom if dx < 0 else 0), wide
            slot = 6 + 2 * side(dx) + side(dy)
        return pltpu.make_async_remote_copy(
            pack.at[side(dy), pl.ds(src, size)],
            strip.at[side(dy), pl.ds(at, size)],
            halo_send.at[slot],
            halo_recv.at[slot],
            device_id={"gx": gx + dx, "gy": gy + dy},
            device_id_type=MESH,
        )

    for dx, dy, ok in near:
        if dy == 0:

            @pl.when(ok)
            def _():
                for copy in row_copies(dx):
                    copy.start()

    load_s.wait()
    load_d.wait()
    lane = lax.broadcasted_iota(jnp.int32, (rows, LANES), 1)
    s_last = s_ext[pl.ds(s_top, rows), pl.ds(right - LANES, LANES)]
    d_last = d_ext[pl.ds(d_top, rows), pl.ds(right - LANES, LANES)]
    pack[0] = jnp.where(lane >= wide, s_last, pltpu.roll(d_last, wide, 1))
    s_first = s_ext[pl.ds(s_top, rows), pl.ds(left, LANES)]
    d_first = d_ext[pl.ds(d_top, rows), pl.ds(left, LANES)]
    pack[1] = jnp.where(lane < wide, s_first, pltpu.roll(d_first, wide, 1))

    for dx, dy, ok in near:
        if dy != 0:

            @pl.when(ok)
            def _():
                col_copy(dx, dy).start()

    for dx, dy, ok in near:
        if dy == 0:

            @pl.when(jnp.logical_not(ok))
            def _():
                at = 0 if dx < 0 else s_bottom
                s_ext[pl.ds(at, wide), pl.ds(left, cols)] = jnp.zeros((wide, cols), jnp.float32)

        else:

            @pl.when(jnp.logical_not(ok))
            def _():
                at = s_top if dx == 0 else (0 if dx < 0 else s_bottom)
                size = rows if dx == 0 else wide
                strip[0 if dy < 0 else 1, pl.ds(at, size)] = jnp.zeros(
                    (size, LANES), jnp.float32
                )

    for dx, dy, ok in near:
        @pl.when(ok)
        def _():
            if dy == 0:
                for copy in row_copies(-dx):
                    copy.wait_recv()
            else:
                col_copy(-dx, -dy).wait_recv()

    s_ext[:, pl.ds(0, LANES)] = strip[0]
    s_ext[:, pl.ds(right, LANES)] = strip[1]
    mid = rows + wide
    d_ext[:, pl.ds(0, LANES)] = pltpu.roll(strip[0, pl.ds(HALF, mid)], wide, 1)
    d_ext[:, pl.ds(right, LANES)] = pltpu.roll(strip[1, pl.ds(HALF, mid)], wide, 1)

    frame = cols + 2 * LANES

    def row_pass1(block, carry):
        at = pl.ds(pl.multiple_of(block * BLOCK, BLOCK), BLOCK)
        high, low = split(s_ext[:, at])
        out = dot3(brow1[0], brow1[1], high, low)
        y_high[:, at], y_low[:, at] = split(out)
        return carry

    lax.fori_loop(0, frame // BLOCK, row_pass1, 0)

    def col_pass(count, base, first, size_in, size_out):
        source = pl.ds(base, size_in)
        b_high = bcol[0, pl.ds(first, size_in), pl.ds(0, size_out)]
        b_low = bcol[1, pl.ds(first, size_in), pl.ds(0, size_out)]
        return dot3(y_high[pl.ds(0, count), source], y_low[pl.ds(0, count), source], b_high, b_low)

    def u_block(block, carry):
        base = pl.multiple_of(block * BLOCK, BLOCK)
        at = pl.ds(pl.multiple_of(base + LANES, LANES), BLOCK)
        kv = col_pass(mid, base, 0, 2 * BLOCK, BLOCK)
        u_high[:, at], u_low[:, at] = split(d_ext[:, at] / kv)
        return carry

    lax.fori_loop(0, cols // BLOCK, u_block, 0)

    lane = lax.broadcasted_iota(jnp.int32, (mid, LANES), 1)
    for at, base, first, keep in (
        (0, 0, LANES, (lane >= LANES - HALF) & (gy > 0)),
        (right, right - LANES, 0, (lane < HALF) & (gy < ngy - 1)),
    ):
        kv = col_pass(mid, base, first, BLOCK, LANES)
        value = jnp.where(keep, d_ext[:, pl.ds(at, LANES)] / kv, jnp.float32(0.0))
        u_high[:, pl.ds(at, LANES)], u_low[:, pl.ds(at, LANES)] = split(value)

    for edge, at in ((gx == 0, 0), (gx == ngx - 1, d_bottom)):

        @pl.when(edge)
        def _():
            zero = jnp.zeros((HALF, frame), jnp.bfloat16)
            u_high[pl.ds(at, HALF), :] = zero
            u_low[pl.ds(at, HALF), :] = zero

    def row_pass2(block, carry):
        at = pl.ds(pl.multiple_of(block * BLOCK, BLOCK), BLOCK)
        out = dot3(brow2[0], brow2[1], u_high[:, at], u_low[:, at])
        y_high[pl.ds(0, rows), at], y_low[pl.ds(0, rows), at] = split(out)
        return carry

    lax.fori_loop(0, frame // BLOCK, row_pass2, 0)

    weight = w_ref[0]

    def ku_block(block, carry):
        base = pl.multiple_of(block * BLOCK, BLOCK)
        ku = col_pass(rows, base, 0, 2 * BLOCK, BLOCK)
        ku_ref[:, pl.ds(base, BLOCK)] = ku
        inner = s_ext[
            pl.ds(s_top, rows), pl.ds(pl.multiple_of(base + LANES, LANES), BLOCK)
        ]
        term[:, pl.ds(base, BLOCK)] = weight * jnp.log(inner * ku)
        return carry

    lax.fori_loop(0, cols // BLOCK, ku_block, 0)

    size = rows // n
    width = cols // SUBS
    far, close = n // 2, (n - 1) // 2
    after, before = lax.rem(z + 1, n), lax.rem(z + n - 1, n)

    def chunk(d):
        return pl.ds(pl.multiple_of(lax.rem(d + 2 * n, n) * size, 8), size)

    def lanes(sub):
        return pl.ds(sub * width, width)

    def cw_copy(src, step, sub):
        return pltpu.make_async_remote_copy(
            src,
            cw.at[step, :, lanes(sub)],
            cw_send.at[step, sub],
            cw_recv.at[step, sub],
            device_id={"map": after},
            device_id_type=MESH,
        )

    def ccw_copy(src, step, sub):
        return pltpu.make_async_remote_copy(
            src,
            ccw.at[step, :, lanes(sub)],
            ccw_send.at[step, sub],
            ccw_recv.at[step, sub],
            device_id={"map": before},
            device_id_type=MESH,
        )

    def cw_next(step, sub):
        cw_copy(cw.at[step - 1, :, lanes(sub)], step - 1, sub).wait_recv()
        cw[step - 1, :, lanes(sub)] += term[chunk(z + far - step), lanes(sub)]
        cw_copy(cw.at[step - 1, :, lanes(sub)], step, sub).start()

    def ccw_next(step, sub):
        ccw_copy(ccw.at[step - 1, :, lanes(sub)], step - 1, sub).wait_recv()
        ccw[step - 1, :, lanes(sub)] += term[chunk(z - close + step), lanes(sub)]
        ccw_copy(ccw.at[step - 1, :, lanes(sub)], step, sub).start()

    for sub in range(SUBS):
        cw_copy(term.at[chunk(z + far), lanes(sub)], 0, sub).start()
        if close > 0:
            ccw_copy(term.at[chunk(z - close), lanes(sub)], 0, sub).start()

    def ring(step, carry):
        for sub in range(SUBS):
            cw_next(step, sub)
            ccw_next(step, sub)
        return carry

    lax.fori_loop(1, close, ring, 0)
    for step in range(max(close, 1), far):
        for sub in range(SUBS):
            cw_next(step, sub)

    def acw_copy(step, sub):
        ref = raw_ref.at[chunk(z - step), lanes(sub)]
        return pltpu.make_async_remote_copy(
            ref,
            ref,
            acw_send.at[step, sub],
            acw_recv.at[step, sub],
            device_id={"map": after},
            device_id_type=MESH,
        )

    def accw_copy(step, sub):
        ref = raw_ref.at[chunk(z + step), lanes(sub)]
        return pltpu.make_async_remote_copy(
            ref,
            ref,
            accw_send.at[step, sub],
            accw_recv.at[step, sub],
            device_id={"map": before},
            device_id_type=MESH,
        )

    partial = jnp.zeros((8, LANES), jnp.float32)
    for sub in range(SUBS):
        cw_copy(cw.at[far - 1, :, lanes(sub)], far - 1, sub).wait_recv()
        value = term[chunk(z), lanes(sub)] + cw[far - 1, :, lanes(sub)]
        if close > 0:
            ccw_copy(ccw.at[close - 1, :, lanes(sub)], close - 1, sub).wait_recv()
            value = value + ccw[close - 1, :, lanes(sub)]
        value = jnp.exp(value)
        raw_ref[chunk(z), lanes(sub)] = value
        acw_copy(0, sub).start()
        if close > 0:
            accw_copy(0, sub).start()
        for i in range(size // 8):
            for j in range(width // LANES):
                partial = partial + value[
                    i * 8 : (i + 1) * 8, j * LANES : (j + 1) * LANES
                ]

    def mass_copies(stage, axis, me, count, slots, sems):
        return [
            pltpu.make_async_remote_copy(
                m_out.at[stage],
                slots.at[me],
                sems.at[0, k],
                sems.at[1, me],
                device_id={axis: lax.rem(me + k, count)},
                device_id_type=MESH,
            )
            for k in range(1, count)
        ]

    def mass_start(stage, axis, me, count, slots, sems, value):
        m_out[stage] = value
        slots[me] = value
        for copy in mass_copies(stage, axis, me, count, slots, sems):
            copy.start()

    def mass_finish(stage, axis, me, count, slots, sems):
        for k in range(1, count):
            source = lax.rem(me + k, count)
            pltpu.make_async_remote_copy(
                m_out.at[stage],
                slots.at[source],
                sems.at[0, k],
                sems.at[1, source],
                device_id={axis: source},
                device_id_type=MESH,
            ).wait_recv()
        total = slots[0]
        for i in range(1, count):
            total = total + slots[i]
        return total

    stages = (
        (0, "gx", gx, ngx, m_gx, m_gx_sem),
        (1, "gy", gy, ngy, m_gy, m_gy_sem),
        (2, "map", z, n, m_map, m_map_sem),
    )

    def gather_step(step, carry):
        for sub in range(SUBS):
            acw_copy(step - 1, sub).wait_recv()
            acw_copy(step, sub).start()
            accw_copy(step - 1, sub).wait_recv()
            accw_copy(step, sub).start()
        return carry

    mass_start(*stages[0], partial)
    third = max(1, (close - 1) // 3)
    points = [1, min(1 + third, close), min(1 + 2 * third, close), close]
    for i in range(3):
        lax.fori_loop(points[i], points[i + 1], gather_step, 0)
        total = mass_finish(*stages[i])
        if i < 2:
            mass_start(*stages[i + 1], total)
    for step in range(max(close, 1), far):
        for sub in range(SUBS):
            acw_copy(step - 1, sub).wait_recv()
            acw_copy(step, sub).start()
    for sub in range(SUBS):
        acw_copy(far - 1, sub).wait_recv()
        if close > 0:
            accw_copy(close - 1, sub).wait_recv()

    cells = float(rows * cols * ngx * ngy)
    norm_ref[...] = jnp.full((8, LANES), cells, jnp.float32) / jnp.sum(total)

    for dx, dy, ok in near:

        @pl.when(ok)
        def _():
            if dy == 0:
                for copy in row_copies(dx):
                    copy.wait_send()
            else:
                col_copy(dx, dy).wait_send()

    def drain_cw(step, carry):
        for sub in range(SUBS):
            cw_copy(cw.at[0, :, lanes(sub)], step, sub).wait_send()
            acw_copy(step, sub).wait_send()
        return carry

    def drain_ccw(step, carry):
        for sub in range(SUBS):
            ccw_copy(ccw.at[0, :, lanes(sub)], step, sub).wait_send()
            accw_copy(step, sub).wait_send()
        return carry

    lax.fori_loop(0, far, drain_cw, 0)
    lax.fori_loop(0, close, drain_ccw, 0)
    for stage in stages:
        for copy in mass_copies(*stage):
            copy.wait_send()


def step(sizes, densities, scaling, weights):
    n, ngx, ngy = sizes
    _, rows, cols = densities.shape
    wide = 2 * HALF
    frame = cols + 2 * LANES
    far, close = n // 2, max((n - 1) // 2, 1)
    size = rows // n
    brow1 = jnp.asarray(band(rows + wide, rows + 2 * wide, HALF))
    brow2 = jnp.asarray(band(rows, rows + wide, HALF))
    bcol = jnp.asarray(np.swapaxes(band(BLOCK, 2 * BLOCK, LANES), 1, 2))
    field = jax.ShapeDtypeStruct((rows, cols), jnp.float32)
    vmem = pl.BlockSpec(memory_space=pltpu.VMEM)
    hbm = pl.BlockSpec(memory_space=pl.ANY)
    dma = pltpu.SemaphoreType.DMA
    f32, bf16 = jnp.float32, jnp.bfloat16
    raw, ku, norm = pl.pallas_call(
        functools.partial(kernel, sizes, rows, cols),
        out_shape=(field, field, jax.ShapeDtypeStruct((8, LANES), f32)),
        in_specs=[hbm, hbm, pl.BlockSpec(memory_space=pltpu.SMEM), vmem, vmem, vmem],
        out_specs=(vmem, vmem, vmem),
        scratch_shapes=[
            pltpu.VMEM((rows + 2 * wide, frame), f32),
            pltpu.VMEM((rows + wide, frame), f32),
            pltpu.VMEM((rows + wide, frame), bf16),
            pltpu.VMEM((rows + wide, frame), bf16),
            pltpu.VMEM((rows + wide, frame), bf16),
            pltpu.VMEM((rows + wide, frame), bf16),
            pltpu.VMEM((rows, cols), f32),
            pltpu.VMEM((2, rows, LANES), f32),
            pltpu.VMEM((2, rows + 2 * wide, LANES), f32),
            pltpu.VMEM((far, size, cols), f32),
            pltpu.VMEM((close, size, cols), f32),
            pltpu.VMEM((3, 8, LANES), f32),
            pltpu.VMEM((ngx, 8, LANES), f32),
            pltpu.VMEM((ngy, 8, LANES), f32),
            pltpu.VMEM((n, 8, LANES), f32),
            dma((2,)),
            dma((10,)),
            dma((10,)),
            dma((far, SUBS)),
            dma((far, SUBS)),
            dma((close, SUBS)),
            dma((close, SUBS)),
            dma((far, SUBS)),
            dma((far, SUBS)),
            dma((close, SUBS)),
            dma((close, SUBS)),
            dma((2, ngx)),
            dma((2, ngy)),
            dma((2, n)),
        ],
        compiler_params=pltpu.CompilerParams(
            collective_id=0, has_side_effects=True, vmem_limit_bytes=48 * 1024 * 1024
        ),
        name="sinkhorn",
    )(scaling, densities, weights, brow1, brow2, bcol)
    barycenter = raw * norm[0, 0]
    new_scaling = barycenter / ku
    return barycenter, new_scaling[None]


def solution(mesh):
    placed = (P("map", "gx", "gy"), P("map", "gx", "gy"), P("map"))
    sizes = (mesh.shape["map"], mesh.shape["gx"], mesh.shape["gy"])
    return jax.shard_map(
        functools.partial(step, sizes),
        mesh=mesh,
        in_specs=placed,
        out_specs=(P("gx", "gy"), P("map", "gx", "gy")),
        check_vma=False,
    )
```

```python
import functools

import jax
import jax.numpy as jnp
import numpy as np
from jax import lax
from jax.experimental import pallas as pl
from jax.experimental.pallas import tpu as pltpu
from jax.sharding import PartitionSpec as P

HALF = 32
SIGMA = 16
LANES = 128
BLOCK = 256
SUBS = 4
WINDOW = 4
MESH = pl.DeviceIdType.MESH


TAPS = np.arange(-HALF, HALF + 1, dtype=np.float64)
TOTAL = float(np.sum(np.exp(-TAPS * TAPS / (2.0 * SIGMA * SIGMA))))


def band(shape, shift):
    offset = (
        lax.broadcasted_iota(jnp.int32, shape, 1)
        - lax.broadcasted_iota(jnp.int32, shape, 0)
        + shift
    )
    distance = offset.astype(jnp.float32)
    values = jnp.exp(distance * distance * (-1.0 / (2.0 * SIGMA * SIGMA))) * (1.0 / TOTAL)
    return split(jnp.where(jnp.abs(offset) <= HALF, values, jnp.float32(0.0)))


def split(x):
    high = x.astype(jnp.bfloat16)
    low = (x - high.astype(jnp.float32)).astype(jnp.bfloat16)
    return high, low


def dot(a, b):
    return jnp.dot(a, b, preferred_element_type=jnp.float32)


def dot3(a_high, a_low, b_high, b_low):
    return dot(a_high, b_high) + (dot(a_high, b_low) + dot(a_low, b_high))


def kernel(
    sizes,
    rows,
    cols,
    s_hbm,
    d_hbm,
    w_ref,
    raw_ref,
    ku_ref,
    norm_ref,
    brow,
    bedge,
    bcol,
    field,
    dens,
    edge,
    pack,
    strip,
    corner,
    y_high,
    y_low,
    y_edge,
    term,
    long,
    short,
    m_out,
    m_gx,
    m_gy,
    m_map,
    in_sem,
    halo_send,
    halo_recv,
    long_send,
    long_recv,
    short_send,
    short_recv,
    along_send,
    along_recv,
    ashort_send,
    ashort_recv,
    m_gx_sem,
    m_gy_sem,
    m_map_sem,
):
    n, ngx, ngy = sizes
    z, gx, gy = lax.axis_index("map"), lax.axis_index("gx"), lax.axis_index("gy")
    main = pl.ds(0, cols)
    quarter = rows // 4
    low_rows, high_rows = pl.ds(0, HALF), pl.ds(rows - HALF, HALF)
    first_tile, last_tile = pl.ds(0, LANES), pl.ds(cols - LANES, LANES)
    halo_tile = pl.ds(cols, LANES)

    load_s = pltpu.make_async_copy(s_hbm.at[0], field.at[0, :, main], in_sem.at[0])
    load_d = pltpu.make_async_copy(d_hbm.at[0], dens, in_sem.at[1])
    load_s.start()
    load_d.start()

    near = []
    for dx in (-1, 0, 1):
        for dy in (-1, 0, 1):
            if dx or dy:
                ok = (gx + dx >= 0) & (gx + dx < ngx) & (gy + dy >= 0) & (gy + dy < ngy)
                near.append((dx, dy, ok))

    barrier = pltpu.get_barrier_semaphore()
    expected = jnp.int32(0)
    for dx, dy, ok in near:
        expected = expected + ok.astype(jnp.int32)

        @pl.when(ok)
        def _():
            pl.semaphore_signal(
                barrier, inc=1, device_id={"gx": gx + dx, "gy": gy + dy}, device_id_type=MESH
            )

    for axis, me, count in (("gx", gx, ngx), ("gy", gy, ngy), ("map", z, n)):
        for k in range(1, count):
            pl.semaphore_signal(
                barrier,
                inc=1,
                device_id={axis: lax.rem(me + k, count)},
                device_id_type=MESH,
            )
        expected = expected + (count - 1)

    def slot(delta):
        return 0 if delta < 0 else 1

    for dx, dy, ok in near:

        @pl.when(jnp.logical_not(ok))
        def _():
            for phase in range(2):
                if dy == 0:
                    edge[phase, slot(dx), :, main] = jnp.zeros((HALF, cols), jnp.float32)
                elif dx == 0:
                    strip[phase, slot(dy)] = jnp.zeros((quarter, LANES), jnp.float32)
                else:
                    corner[phase, slot(dx), slot(dy)] = jnp.zeros((HALF, LANES), jnp.float32)

    pl.semaphore_wait(barrier, expected)

    def halo_copy(phase, dx, dy):
        if dy == 0:
            source = s_hbm.at[0] if phase == 0 else field.at[1, :, main]
            source = source.at[low_rows if dx < 0 else high_rows]
            target = edge.at[phase, slot(-dx), :, main]
            index = slot(dx)
        elif dx == 0:
            source = pack.at[phase, slot(dy)]
            target = strip.at[phase, slot(-dy)]
            index = 2 + slot(dy)
        else:
            source = field.at[
                phase, low_rows if dx < 0 else high_rows, first_tile if dy < 0 else last_tile
            ]
            target = corner.at[phase, slot(-dx), slot(-dy)]
            index = 4 + 2 * slot(dx) + slot(dy)
        return pltpu.make_async_remote_copy(
            source,
            target,
            halo_send.at[phase, index],
            halo_recv.at[phase, index],
            device_id={"gx": gx + dx, "gy": gy + dy},
            device_id_type=MESH,
        )

    def halo_start(phase, which):
        for dx, dy, ok in near:
            if which(dx, dy):

                @pl.when(ok)
                def _():
                    halo_copy(phase, dx, dy).start()

    lane = lax.broadcasted_iota(jnp.int32, (quarter, LANES), 1)

    def rolled(value, shift):
        return pltpu.roll(value, shift % LANES, 1) if shift % LANES else value

    def pack_strips(phase):
        for q in range(4):
            at = pl.ds(q * quarter, quarter)
            here = (lane >= q * HALF) & (lane < (q + 1) * HALF)
            begin = rolled(field[phase, at, first_tile], q * HALF)
            end = rolled(field[phase, at, last_tile], (q + 1) * HALF)
            if q == 0:
                begin_all, end_all = begin, end
            else:
                begin_all = jnp.where(here, begin, begin_all)
                end_all = jnp.where(here, end, end_all)
        pack[phase, 0] = begin_all
        pack[phase, 1] = end_all

    def joined(left, right, lane):
        zero = jnp.float32(0.0)
        return jnp.where(lane >= LANES - HALF, left, jnp.where(lane < HALF, right, zero))

    def halo_finish(phase):
        for dx, dy, ok in near:
            @pl.when(ok)
            def _():
                halo_copy(phase, -dx, -dy).wait_recv()

        for q in range(4):
            left = rolled(strip[phase, 0], -(q + 1) * HALF)
            right = rolled(strip[phase, 1], -q * HALF)
            field[phase, pl.ds(q * quarter, quarter), halo_tile] = joined(left, right, lane)
        lane_corner = lax.broadcasted_iota(jnp.int32, (HALF, LANES), 1)
        for above in range(2):
            edge[phase, above, :, halo_tile] = joined(
                corner[phase, above, 0], corner[phase, above, 1], lane_corner
            )

    frame = cols + 2 * LANES

    def put(at_rows, at_cols, value):
        y_high[at_rows, at_cols], y_low[at_rows, at_cols] = split(value)

    def row_own(phase):
        def body(block, carry):
            base = pl.multiple_of(block * BLOCK, BLOCK)
            at = pl.ds(base, BLOCK)
            out = dot3(brow[0], brow[1], *split(field[phase, :, at]))
            put(pl.ds(0, rows), pl.ds(pl.multiple_of(base + LANES, LANES), BLOCK), out)
            y_edge[0, :, at] = out[:HALF]
            y_edge[1, :, at] = out[rows - HALF :]
            return carry

        lax.fori_loop(0, cols // BLOCK, body, 0)

    def row_halo(phase):
        out = dot3(brow[0], brow[1], *split(field[phase, :, halo_tile]))
        y_edge[0, :, halo_tile] = out[:HALF]
        y_edge[1, :, halo_tile] = out[rows - HALF :]
        for at in (0, cols + LANES):
            put(pl.ds(0, rows), pl.ds(at, LANES), out)
        for above, at_rows in ((0, low_rows), (1, high_rows)):
            more = dot3(bedge[above, 0], bedge[above, 1], *split(edge[phase, above]))
            total = y_edge[above] + more
            put(at_rows, pl.ds(LANES, cols + LANES), total)
            put(at_rows, pl.ds(0, LANES), total[:, cols:])

    def col_pass(base):
        source = pl.ds(base, 2 * BLOCK)
        return dot3(y_high[:, source], y_low[:, source], bcol[0], bcol[1])

    halo_start(0, lambda dx, dy: dy == 0)
    load_s.wait()
    pack_strips(0)
    halo_start(0, lambda dx, dy: dy != 0)
    brow[0], brow[1] = band((rows, rows), 0)
    for above, shift in ((0, -HALF), (1, HALF)):
        bedge[above, 0], bedge[above, 1] = band((HALF, HALF), shift)
    bcol[0], bcol[1] = band((2 * BLOCK, BLOCK), LANES)
    row_own(0)
    halo_finish(0)
    row_halo(0)
    load_d.wait()

    def u_block(block, carry):
        base = pl.multiple_of(block * BLOCK, BLOCK)
        at = pl.ds(base, BLOCK)
        field[1, :, at] = dens[:, at] / col_pass(base)
        return carry

    lax.fori_loop(0, cols // BLOCK, u_block, 0)
    halo_start(1, lambda dx, dy: dy == 0)
    pack_strips(1)
    halo_start(1, lambda dx, dy: dy != 0)
    row_own(1)
    halo_finish(1)
    row_halo(1)
    weight = w_ref[0]

    def ku_block(block, carry):
        base = pl.multiple_of(block * BLOCK, BLOCK)
        at = pl.ds(base, BLOCK)
        ku = col_pass(base)
        ku_ref[:, at] = ku
        term[:, at] = weight * jnp.log(field[0, :, at] * ku)
        return carry

    lax.fori_loop(0, cols // BLOCK, ku_block, 0)

    size = rows // n
    width = cols // SUBS
    far, close = n // 2, (n - 1) // 2
    after, before = lax.rem(z + 1, n), lax.rem(z + n - 1, n)

    def chunk(d):
        return pl.ds(pl.multiple_of(lax.rem(d + 2 * n, n) * size, 8), size)

    def lanes(sub):
        return pl.ds(sub * width, width)

    def target(sub, up):
        return {"map": after if (sub % 2 == 0) == up else before}

    def toward(sub, hops):
        return z + hops if sub % 2 == 0 else z - hops

    def long_copy(src, step, sub):
        return pltpu.make_async_remote_copy(
            src,
            long.at[step, :, lanes(sub)],
            long_send.at[step, sub],
            long_recv.at[step, sub],
            device_id=target(sub, True),
            device_id_type=MESH,
        )

    def short_copy(src, step, sub):
        return pltpu.make_async_remote_copy(
            src,
            short.at[step, :, lanes(sub)],
            short_send.at[step, sub],
            short_recv.at[step, sub],
            device_id=target(sub, False),
            device_id_type=MESH,
        )

    def long_next(step, sub):
        ref = long.at[step - 1, :, lanes(sub)]
        long_copy(ref, step - 1, sub).wait_recv()
        ref[...] += term[chunk(toward(sub, far - step)), lanes(sub)]
        return long_copy(ref, step, sub)

    def short_next(step, sub):
        ref = short.at[step - 1, :, lanes(sub)]
        short_copy(ref, step - 1, sub).wait_recv()
        ref[...] += term[chunk(toward(sub, step - close)), lanes(sub)]
        return short_copy(ref, step, sub)

    def send(step, sub, copy, same):
        back = sub - WINDOW
        if back >= 0:
            same(step, back).wait_send()
        else:
            @pl.when(step > 0)
            def _():
                same(step - 1, back + SUBS).wait_send()
        copy.start()

    def long_left(step, sub):
        return long_copy(long.at[0, :, lanes(sub)], step, sub)

    def short_left(step, sub):
        return short_copy(short.at[0, :, lanes(sub)], step, sub)

    for sub in range(SUBS):
        send(0, sub, long_copy(term.at[chunk(toward(sub, far)), lanes(sub)], 0, sub), long_left)
        send(0, sub, short_copy(term.at[chunk(toward(sub, -close)), lanes(sub)], 0, sub), short_left)

    def ring(step, carry):
        for sub in range(SUBS):
            send(step, sub, long_next(step, sub), long_left)
            send(step, sub, short_next(step, sub), short_left)
        return carry

    lax.fori_loop(1, close, ring, 0)
    for step in range(close, far):
        for sub in range(SUBS):
            send(step, sub, long_next(step, sub), long_left)

    def along_copy(step, sub):
        ref = raw_ref.at[chunk(toward(sub, -step)), lanes(sub)]
        return pltpu.make_async_remote_copy(
            ref,
            ref,
            along_send.at[step, sub],
            along_recv.at[step, sub],
            device_id=target(sub, True),
            device_id_type=MESH,
        )

    def ashort_copy(step, sub):
        ref = raw_ref.at[chunk(toward(sub, step)), lanes(sub)]
        return pltpu.make_async_remote_copy(
            ref,
            ref,
            ashort_send.at[step, sub],
            ashort_recv.at[step, sub],
            device_id=target(sub, False),
            device_id_type=MESH,
        )

    partial = jnp.zeros((8, LANES), jnp.float32)
    for sub in range(SUBS):
        long_left(far - 1, sub).wait_recv()
        short_left(close - 1, sub).wait_recv()
        value = term[chunk(z), lanes(sub)] + long[far - 1, :, lanes(sub)]
        value = jnp.exp(value + short[close - 1, :, lanes(sub)])
        raw_ref[chunk(z), lanes(sub)] = value
        send(0, sub, along_copy(0, sub), along_copy)
        send(0, sub, ashort_copy(0, sub), ashort_copy)
        for i in range(size // 8):
            for j in range(width // LANES):
                partial = partial + value[
                    i * 8 : (i + 1) * 8, j * LANES : (j + 1) * LANES
                ]

    def mass_copies(stage, axis, me, count, slots, sems):
        return [
            pltpu.make_async_remote_copy(
                m_out.at[stage],
                slots.at[me],
                sems.at[0, k],
                sems.at[1, me],
                device_id={axis: lax.rem(me + k, count)},
                device_id_type=MESH,
            )
            for k in range(1, count)
        ]

    def mass_start(stage, axis, me, count, slots, sems, value):
        m_out[stage] = value
        slots[me] = value
        for copy in mass_copies(stage, axis, me, count, slots, sems):
            copy.start()

    def mass_finish(stage, axis, me, count, slots, sems):
        for k in range(1, count):
            source = lax.rem(me + k, count)
            pltpu.make_async_remote_copy(
                m_out.at[stage],
                slots.at[source],
                sems.at[0, k],
                sems.at[1, source],
                device_id={axis: source},
                device_id_type=MESH,
            ).wait_recv()
        total = slots[0]
        for i in range(1, count):
            total = total + slots[i]
        return total

    stages = (
        (0, "gx", gx, ngx, m_gx, m_gx_sem),
        (1, "gy", gy, ngy, m_gy, m_gy_sem),
        (2, "map", z, n, m_map, m_map_sem),
    )

    def gather_step(step, carry):
        for sub in range(SUBS):
            along_copy(step - 1, sub).wait_recv()
            send(step, sub, along_copy(step, sub), along_copy)
            ashort_copy(step - 1, sub).wait_recv()
            send(step, sub, ashort_copy(step, sub), ashort_copy)
        return carry

    mass_start(*stages[0], partial)
    third = max(1, (close - 1) // 3)
    points = [1, min(1 + third, close), min(1 + 2 * third, close), close]
    for i in range(3):
        lax.fori_loop(points[i], points[i + 1], gather_step, 0)
        total = mass_finish(*stages[i])
        if i < 2:
            mass_start(*stages[i + 1], total)
    for step in range(close, far):
        for sub in range(SUBS):
            along_copy(step - 1, sub).wait_recv()
            send(step, sub, along_copy(step, sub), along_copy)
    for sub in range(SUBS):
        along_copy(far - 1, sub).wait_recv()
        ashort_copy(close - 1, sub).wait_recv()

    cells = float(rows * cols * ngx * ngy)
    norm_ref[...] = jnp.full((1, 1), cells, jnp.float32) / jnp.sum(total)

    for phase in range(2):
        for dx, dy, ok in near:

            @pl.when(ok)
            def _():
                halo_copy(phase, dx, dy).wait_send()

    for sub in range(SUBS - WINDOW, SUBS):
        long_left(far - 1, sub).wait_send()
        short_left(close - 1, sub).wait_send()
        along_copy(far - 1, sub).wait_send()
        ashort_copy(close - 1, sub).wait_send()
    for stage in stages:
        for copy in mass_copies(*stage):
            copy.wait_send()


def step(sizes, densities, scaling, weights):
    n, ngx, ngy = sizes
    _, rows, cols = densities.shape
    frame = cols + 2 * LANES
    far, close = n // 2, (n - 1) // 2
    size = rows // n
    out = jax.ShapeDtypeStruct((rows, cols), jnp.float32)
    vmem = pl.BlockSpec(memory_space=pltpu.VMEM)
    hbm = pl.BlockSpec(memory_space=pl.ANY)
    dma = pltpu.SemaphoreType.DMA
    f32, bf16 = jnp.float32, jnp.bfloat16
    raw, ku, norm = pl.pallas_call(
        functools.partial(kernel, sizes, rows, cols),
        out_shape=(out, out, jax.ShapeDtypeStruct((1, 1), f32)),
        in_specs=[hbm, hbm, pl.BlockSpec(memory_space=pltpu.SMEM)],
        out_specs=(vmem, vmem, vmem),
        scratch_shapes=[
            pltpu.VMEM((2, rows, rows), bf16),
            pltpu.VMEM((2, 2, HALF, HALF), bf16),
            pltpu.VMEM((2, 2 * BLOCK, BLOCK), bf16),
            pltpu.VMEM((2, rows, cols + LANES), f32),
            pltpu.VMEM((rows, cols), f32),
            pltpu.VMEM((2, 2, HALF, cols + LANES), f32),
            pltpu.VMEM((2, 2, rows // 4, LANES), f32),
            pltpu.VMEM((2, 2, rows // 4, LANES), f32),
            pltpu.VMEM((2, 2, 2, HALF, LANES), f32),
            pltpu.VMEM((rows, frame), bf16),
            pltpu.VMEM((rows, frame), bf16),
            pltpu.VMEM((2, HALF, cols + LANES), f32),
            pltpu.VMEM((rows, cols), f32),
            pltpu.VMEM((far, size, cols), f32),
            pltpu.VMEM((close, size, cols), f32),
            pltpu.VMEM((3, 8, LANES), f32),
            pltpu.VMEM((ngx, 8, LANES), f32),
            pltpu.VMEM((ngy, 8, LANES), f32),
            pltpu.VMEM((n, 8, LANES), f32),
            dma((2,)),
            dma((2, 8)),
            dma((2, 8)),
            dma((far, SUBS)),
            dma((far, SUBS)),
            dma((close, SUBS)),
            dma((close, SUBS)),
            dma((far, SUBS)),
            dma((far, SUBS)),
            dma((close, SUBS)),
            dma((close, SUBS)),
            dma((2, ngx)),
            dma((2, ngy)),
            dma((2, n)),
        ],
        compiler_params=pltpu.CompilerParams(
            collective_id=0, has_side_effects=True, vmem_limit_bytes=48 * 1024 * 1024
        ),
        name="sinkhorn",
    )(scaling, densities, weights)
    barycenter = raw * norm[0, 0]
    new_scaling = barycenter / ku
    return barycenter, new_scaling[None]


def solution(mesh):
    placed = (P("map", "gx", "gy"), P("map", "gx", "gy"), P("map"))
    sizes = (mesh.shape["map"], mesh.shape["gx"], mesh.shape["gy"])
    return jax.shard_map(
        functools.partial(step, sizes),
        mesh=mesh,
        in_specs=placed,
        out_specs=(P("gx", "gy"), P("map", "gx", "gy")),
        check_vma=False,
    )
```

```python
import functools

import jax
import jax.numpy as jnp
import numpy as np
from jax import lax
from jax.experimental import pallas as pl
from jax.experimental.pallas import tpu as pltpu
from jax.sharding import PartitionSpec as P

HALF = 32
SIGMA = 16
LANES = 128
BLOCK = 256
SUBS = 4
SKIPS = (2, 1)
MESH = pl.DeviceIdType.MESH


TAPS = np.arange(-HALF, HALF + 1, dtype=np.float64)
TOTAL = float(np.sum(np.exp(-TAPS * TAPS / (2.0 * SIGMA * SIGMA))))


def band(shape, shift):
    offset = (
        lax.broadcasted_iota(jnp.int32, shape, 1)
        - lax.broadcasted_iota(jnp.int32, shape, 0)
        + shift
    )
    distance = offset.astype(jnp.float32)
    values = jnp.exp(distance * distance * (-1.0 / (2.0 * SIGMA * SIGMA))) * (1.0 / TOTAL)
    return split(jnp.where(jnp.abs(offset) <= HALF, values, jnp.float32(0.0)))


def split(x):
    high = x.astype(jnp.bfloat16)
    low = (x - high.astype(jnp.float32)).astype(jnp.bfloat16)
    return high, low


def dot(a, b):
    return jnp.dot(a, b, preferred_element_type=jnp.float32)


def dot3(a_high, a_low, b_high, b_low):
    return dot(a_high, b_high) + (dot(a_high, b_low) + dot(a_low, b_high))


def kernel(
    sizes,
    rows,
    cols,
    s_hbm,
    d_hbm,
    w_ref,
    raw_ref,
    ku_ref,
    norm_ref,
    brow,
    bedge,
    bcol,
    field,
    dens,
    edge,
    pack,
    strip,
    corner,
    y_high,
    y_low,
    y_edge,
    term,
    sums0,
    sums1,
    asides0,
    asides1,
    m_out,
    m_gx,
    m_gy,
    m_map,
    in_sem,
    halo_send,
    halo_recv,
    sum_sem0,
    sum_sem1,
    aside_sem0,
    aside_sem1,
    all_sem0,
    all_sem1,
    leaf_sem0,
    leaf_sem1,
    m_gx_sem,
    m_gy_sem,
    m_map_sem,
):
    n, ngx, ngy = sizes
    z, gx, gy = lax.axis_index("map"), lax.axis_index("gx"), lax.axis_index("gy")
    main = pl.ds(0, cols)
    quarter = rows // 4
    low_rows, high_rows = pl.ds(0, HALF), pl.ds(rows - HALF, HALF)
    first_tile, last_tile = pl.ds(0, LANES), pl.ds(cols - LANES, LANES)
    halo_tile = pl.ds(cols, LANES)

    load_s = pltpu.make_async_copy(s_hbm.at[0], field.at[0, :, main], in_sem.at[0])
    load_d = pltpu.make_async_copy(d_hbm.at[0], dens, in_sem.at[1])
    load_s.start()
    load_d.start()

    near = []
    for dx in (-1, 0, 1):
        for dy in (-1, 0, 1):
            if dx or dy:
                ok = (gx + dx >= 0) & (gx + dx < ngx) & (gy + dy >= 0) & (gy + dy < ngy)
                near.append((dx, dy, ok))

    barrier = pltpu.get_barrier_semaphore()
    expected = jnp.int32(0)
    for dx, dy, ok in near:
        expected = expected + ok.astype(jnp.int32)

        @pl.when(ok)
        def _():
            pl.semaphore_signal(
                barrier, inc=1, device_id={"gx": gx + dx, "gy": gy + dy}, device_id_type=MESH
            )

    for axis, me, count in (("gx", gx, ngx), ("gy", gy, ngy), ("map", z, n)):
        for k in range(1, count):
            pl.semaphore_signal(
                barrier,
                inc=1,
                device_id={axis: lax.rem(me + k, count)},
                device_id_type=MESH,
            )
        expected = expected + (count - 1)

    def slot(delta):
        return 0 if delta < 0 else 1

    for dx, dy, ok in near:

        @pl.when(jnp.logical_not(ok))
        def _():
            for phase in range(2):
                if dy == 0:
                    edge[phase, slot(dx), :, main] = jnp.zeros((HALF, cols), jnp.float32)
                elif dx == 0:
                    strip[phase, slot(dy)] = jnp.zeros((quarter, LANES), jnp.float32)
                else:
                    corner[phase, slot(dx), slot(dy)] = jnp.zeros((HALF, LANES), jnp.float32)

    pl.semaphore_wait(barrier, expected)

    def halo_copy(phase, dx, dy):
        if dy == 0:
            source = s_hbm.at[0] if phase == 0 else field.at[1, :, main]
            source = source.at[low_rows if dx < 0 else high_rows]
            target = edge.at[phase, slot(-dx), :, main]
            index = slot(dx)
        elif dx == 0:
            source = pack.at[phase, slot(dy)]
            target = strip.at[phase, slot(-dy)]
            index = 2 + slot(dy)
        else:
            source = field.at[
                phase, low_rows if dx < 0 else high_rows, first_tile if dy < 0 else last_tile
            ]
            target = corner.at[phase, slot(-dx), slot(-dy)]
            index = 4 + 2 * slot(dx) + slot(dy)
        return pltpu.make_async_remote_copy(
            source,
            target,
            halo_send.at[phase, index],
            halo_recv.at[phase, index],
            device_id={"gx": gx + dx, "gy": gy + dy},
            device_id_type=MESH,
        )

    def halo_start(phase, which):
        for dx, dy, ok in near:
            if which(dx, dy):

                @pl.when(ok)
                def _():
                    halo_copy(phase, dx, dy).start()

    lane = lax.broadcasted_iota(jnp.int32, (quarter, LANES), 1)

    def rolled(value, shift):
        return pltpu.roll(value, shift % LANES, 1) if shift % LANES else value

    def pack_strips(phase):
        for q in range(4):
            at = pl.ds(q * quarter, quarter)
            here = (lane >= q * HALF) & (lane < (q + 1) * HALF)
            begin = rolled(field[phase, at, first_tile], q * HALF)
            end = rolled(field[phase, at, last_tile], (q + 1) * HALF)
            if q == 0:
                begin_all, end_all = begin, end
            else:
                begin_all = jnp.where(here, begin, begin_all)
                end_all = jnp.where(here, end, end_all)
        pack[phase, 0] = begin_all
        pack[phase, 1] = end_all

    def joined(left, right, lane):
        zero = jnp.float32(0.0)
        return jnp.where(lane >= LANES - HALF, left, jnp.where(lane < HALF, right, zero))

    def halo_finish(phase):
        for dx, dy, ok in near:
            @pl.when(ok)
            def _():
                halo_copy(phase, -dx, -dy).wait_recv()

        for q in range(4):
            left = rolled(strip[phase, 0], -(q + 1) * HALF)
            right = rolled(strip[phase, 1], -q * HALF)
            field[phase, pl.ds(q * quarter, quarter), halo_tile] = joined(left, right, lane)
        lane_corner = lax.broadcasted_iota(jnp.int32, (HALF, LANES), 1)
        for above in range(2):
            edge[phase, above, :, halo_tile] = joined(
                corner[phase, above, 0], corner[phase, above, 1], lane_corner
            )

    frame = cols + 2 * LANES

    def put(at_rows, at_cols, value):
        y_high[at_rows, at_cols], y_low[at_rows, at_cols] = split(value)

    def row_own(phase):
        def body(block, carry):
            base = pl.multiple_of(block * BLOCK, BLOCK)
            at = pl.ds(base, BLOCK)
            out = dot3(brow[0], brow[1], *split(field[phase, :, at]))
            put(pl.ds(0, rows), pl.ds(pl.multiple_of(base + LANES, LANES), BLOCK), out)
            y_edge[0, :, at] = out[:HALF]
            y_edge[1, :, at] = out[rows - HALF :]
            return carry

        lax.fori_loop(0, cols // BLOCK, body, 0)

    def row_halo(phase):
        out = dot3(brow[0], brow[1], *split(field[phase, :, halo_tile]))
        y_edge[0, :, halo_tile] = out[:HALF]
        y_edge[1, :, halo_tile] = out[rows - HALF :]
        for at in (0, cols + LANES):
            put(pl.ds(0, rows), pl.ds(at, LANES), out)
        for above, at_rows in ((0, low_rows), (1, high_rows)):
            more = dot3(bedge[above, 0], bedge[above, 1], *split(edge[phase, above]))
            total = y_edge[above] + more
            put(at_rows, pl.ds(LANES, cols + LANES), total)
            put(at_rows, pl.ds(0, LANES), total[:, cols:])

    def col_pass(base):
        source = pl.ds(base, 2 * BLOCK)
        return dot3(y_high[:, source], y_low[:, source], bcol[0], bcol[1])

    halo_start(0, lambda dx, dy: dy == 0)
    load_s.wait()
    pack_strips(0)
    halo_start(0, lambda dx, dy: dy != 0)
    brow[0], brow[1] = band((rows, rows), 0)
    for above, shift in ((0, -HALF), (1, HALF)):
        bedge[above, 0], bedge[above, 1] = band((HALF, HALF), shift)
    bcol[0], bcol[1] = band((2 * BLOCK, BLOCK), LANES)
    row_own(0)
    halo_finish(0)
    row_halo(0)
    load_d.wait()

    def u_block(block, carry):
        base = pl.multiple_of(block * BLOCK, BLOCK)
        at = pl.ds(base, BLOCK)
        field[1, :, at] = dens[:, at] / col_pass(base)
        return carry

    lax.fori_loop(0, cols // BLOCK, u_block, 0)
    halo_start(1, lambda dx, dy: dy == 0)
    pack_strips(1)
    halo_start(1, lambda dx, dy: dy != 0)
    row_own(1)
    halo_finish(1)
    row_halo(1)
    weight = w_ref[0]

    def ku_block(block, carry):
        base = pl.multiple_of(block * BLOCK, BLOCK)
        at = pl.ds(base, BLOCK)
        ku = col_pass(base)
        ku_ref[:, at] = ku
        term[:, at] = weight * jnp.log(field[0, :, at] * ku)
        return carry

    size = rows // n
    width = cols // SUBS
    hops = (n // 2, (n - 1) // 2)
    skips = SKIPS
    plain = [hops[way] - 2 * skips[way] for way in range(2)]
    steps = [hops[way] - skips[way] for way in range(2)]

    def chunk(d):
        return pl.ds(pl.multiple_of(lax.rem(d + 2 * n, n) * size, 8), size)

    def lanes(sub):
        return pl.ds(sub * width, width)

    def toward(way, sub, distance):
        return z + distance if (sub + way) % 2 == 0 else z - distance

    def device(way, sub, distance):
        return {"map": lax.rem(toward(way, sub, distance) + n, n)}

    sums, asides = (sums0, sums1), (asides0, asides1)
    sum_sems, aside_sems = (sum_sem0, sum_sem1), (aside_sem0, aside_sem1)
    all_sems, leaf_sems = (all_sem0, all_sem1), (leaf_sem0, leaf_sem1)

    def remote(source, target, sems, step, sub, to):
        return pltpu.make_async_remote_copy(
            source,
            target,
            sems.at[0, step, sub],
            sems.at[1, step, sub],
            device_id=to,
            device_id_type=MESH,
        )

    def role(way, step):
        if step < plain[way]:
            return hops[way] - step
        return 2 * (skips[way] - (step - plain[way]))

    def sum_copy(way, step, sub, source=None):
        target = sums[way].at[step, :, lanes(sub)]
        source = target if source is None else source
        to = device(way, sub, 1 if step < plain[way] else 2)
        return remote(source, target, sum_sems[way], step, sub, to)

    def aside_copy(way, index, sub):
        source = term.at[chunk(toward(way, sub, 2 * index + 1)), lanes(sub)]
        target = asides[way].at[index, :, lanes(sub)]
        return remote(source, target, aside_sems[way], index, sub, device(way, sub, 1))

    def arrived(way, step, sub):
        sum_copy(way, step - 1, sub).wait_recv()
        value = sums[way][step - 1, :, lanes(sub)]
        if step > plain[way]:
            index = skips[way] - (step - plain[way])
            aside_copy(way, index, sub).wait_recv()
            value = value + asides[way][index, :, lanes(sub)]
        return value

    def sum_first(sub):
        for way in range(2):
            own = term.at[chunk(toward(way, sub, hops[way])), lanes(sub)]
            sum_copy(way, 0, sub, own).start()

    def sum_next(way, step, sub):
        at = chunk(toward(way, sub, role(way, step)))
        held = sums[way].at[step - 1, :, lanes(sub)]
        held[...] = arrived(way, step, sub) + term[at, lanes(sub)]
        sum_copy(way, step, sub, held).start()

    for block in range(cols // BLOCK):
        ku_block(block, 0)
        for sub in range(SUBS):
            if block * BLOCK < (sub + 1) * width <= (block + 1) * BLOCK:
                sum_first(sub)

    for sub in range(SUBS):
        for way in range(2):
            for index in range(skips[way]):
                aside_copy(way, index, sub).start()
    for step in range(1, max(steps)):
        for sub in range(SUBS):
            for way in range(2):
                if step < steps[way]:
                    sum_next(way, step, sub)

    def gather_copy(way, step, sub):
        done = 2 * step if step <= skips[way] else step + skips[way]
        ref = raw_ref.at[chunk(toward(way, sub, -done)), lanes(sub)]
        to = device(way, sub, 2 if step < skips[way] else 1)
        return remote(ref, ref, all_sems[way], step, sub, to)

    def leaf_copy(way, index, sub):
        ref = raw_ref.at[chunk(toward(way, sub, -2 * index)), lanes(sub)]
        return remote(ref, ref, leaf_sems[way], index, sub, device(way, sub, 1))

    def gather_start(way, step, sub):
        gather_copy(way, step, sub).start()
        if step < skips[way]:
            leaf_copy(way, step, sub).start()

    partial = jnp.zeros((8, LANES), jnp.float32)
    for sub in range(SUBS):
        value = term[chunk(z), lanes(sub)] + arrived(0, steps[0], sub)
        value = jnp.exp(value + arrived(1, steps[1], sub))
        raw_ref[chunk(z), lanes(sub)] = value
        for way in range(2):
            gather_start(way, 0, sub)
        for i in range(size // 8):
            for j in range(width // LANES):
                partial = partial + value[
                    i * 8 : (i + 1) * 8, j * LANES : (j + 1) * LANES
                ]

    def mass_copies(stage, axis, me, count, slots, sems):
        return [
            pltpu.make_async_remote_copy(
                m_out.at[stage],
                slots.at[me],
                sems.at[0, k],
                sems.at[1, me],
                device_id={axis: lax.rem(me + k, count)},
                device_id_type=MESH,
            )
            for k in range(1, count)
        ]

    def mass_start(stage, axis, me, count, slots, sems, value):
        m_out[stage] = value
        slots[me] = value
        for copy in mass_copies(stage, axis, me, count, slots, sems):
            copy.start()

    def mass_finish(stage, axis, me, count, slots, sems):
        for k in range(1, count):
            source = lax.rem(me + k, count)
            pltpu.make_async_remote_copy(
                m_out.at[stage],
                slots.at[source],
                sems.at[0, k],
                sems.at[1, source],
                device_id={axis: source},
                device_id_type=MESH,
            ).wait_recv()
        total = slots[0]
        for i in range(1, count):
            total = total + slots[i]
        return total

    stages = (
        (0, "gx", gx, ngx, m_gx, m_gx_sem),
        (1, "gy", gy, ngy, m_gy, m_gy_sem),
        (2, "map", z, n, m_map, m_map_sem),
    )

    mass_start(*stages[0], partial)
    turns = [1 + (i + 1) * (max(steps) - 1) // 3 for i in range(3)]
    for step in range(1, max(steps) + 1):
        for i in range(3):
            if step == turns[i]:
                total = mass_finish(*stages[i])
                if i < 2:
                    mass_start(*stages[i + 1], total)
        for sub in range(SUBS):
            for way in range(2):
                if step <= steps[way]:
                    gather_copy(way, step - 1, sub).wait_recv()
                if step < steps[way]:
                    gather_start(way, step, sub)
    for sub in range(SUBS):
        for way in range(2):
            for index in range(skips[way]):
                leaf_copy(way, index, sub).wait_recv()

    cells = float(rows * cols * ngx * ngy)
    norm_ref[...] = jnp.full((1, 1), cells, jnp.float32) / jnp.sum(total)

    for phase in range(2):
        for dx, dy, ok in near:

            @pl.when(ok)
            def _():
                halo_copy(phase, dx, dy).wait_send()

    for sub in range(SUBS):
        for way in range(2):
            for step in range(steps[way]):
                sum_copy(way, step, sub).wait_send()
                gather_copy(way, step, sub).wait_send()
            for index in range(skips[way]):
                aside_copy(way, index, sub).wait_send()
                leaf_copy(way, index, sub).wait_send()
    for stage in stages:
        for copy in mass_copies(*stage):
            copy.wait_send()


def step(sizes, densities, scaling, weights):
    n, ngx, ngy = sizes
    _, rows, cols = densities.shape
    frame = cols + 2 * LANES
    size = rows // n
    steps = (n // 2 - SKIPS[0], (n - 1) // 2 - SKIPS[1])
    extra = [max(k, 1) for k in SKIPS]
    out = jax.ShapeDtypeStruct((rows, cols), jnp.float32)
    vmem = pl.BlockSpec(memory_space=pltpu.VMEM)
    hbm = pl.BlockSpec(memory_space=pl.ANY)
    dma = pltpu.SemaphoreType.DMA
    f32, bf16 = jnp.float32, jnp.bfloat16
    raw, ku, norm = pl.pallas_call(
        functools.partial(kernel, sizes, rows, cols),
        out_shape=(out, out, jax.ShapeDtypeStruct((1, 1), f32)),
        in_specs=[hbm, hbm, pl.BlockSpec(memory_space=pltpu.SMEM)],
        out_specs=(vmem, vmem, vmem),
        scratch_shapes=[
            pltpu.VMEM((2, rows, rows), bf16),
            pltpu.VMEM((2, 2, HALF, HALF), bf16),
            pltpu.VMEM((2, 2 * BLOCK, BLOCK), bf16),
            pltpu.VMEM((2, rows, cols + LANES), f32),
            pltpu.VMEM((rows, cols), f32),
            pltpu.VMEM((2, 2, HALF, cols + LANES), f32),
            pltpu.VMEM((2, 2, rows // 4, LANES), f32),
            pltpu.VMEM((2, 2, rows // 4, LANES), f32),
            pltpu.VMEM((2, 2, 2, HALF, LANES), f32),
            pltpu.VMEM((rows, frame), bf16),
            pltpu.VMEM((rows, frame), bf16),
            pltpu.VMEM((2, HALF, cols + LANES), f32),
            pltpu.VMEM((rows, cols), f32),
            *[pltpu.VMEM((k, size, cols), f32) for k in (*steps, *extra)],
            pltpu.VMEM((3, 8, LANES), f32),
            pltpu.VMEM((ngx, 8, LANES), f32),
            pltpu.VMEM((ngy, 8, LANES), f32),
            pltpu.VMEM((n, 8, LANES), f32),
            dma((2,)),
            dma((2, 8)),
            dma((2, 8)),
            *[dma((2, k, SUBS)) for k in (*steps, *extra)],
            *[dma((2, k, SUBS)) for k in (*steps, *extra)],
            dma((2, ngx)),
            dma((2, ngy)),
            dma((2, n)),
        ],
        compiler_params=pltpu.CompilerParams(
            collective_id=0, has_side_effects=True, vmem_limit_bytes=48 * 1024 * 1024
        ),
        name="sinkhorn",
    )(scaling, densities, weights)
    barycenter = raw * norm[0, 0]
    new_scaling = barycenter / ku
    return barycenter, new_scaling[None]


def solution(mesh):
    placed = (P("map", "gx", "gy"), P("map", "gx", "gy"), P("map"))
    sizes = (mesh.shape["map"], mesh.shape["gx"], mesh.shape["gy"])
    return jax.shard_map(
        functools.partial(step, sizes),
        mesh=mesh,
        in_specs=placed,
        out_specs=(P("gx", "gy"), P("map", "gx", "gy")),
        check_vma=False,
    )
```

```python
import functools

import jax
import jax.numpy as jnp
import numpy as np
from jax import lax
from jax.experimental import pallas as pl
from jax.experimental.pallas import tpu as pltpu
from jax.sharding import PartitionSpec as P

HALF = 32
SIGMA = 16
LANES = 128
BLOCK = 256
SUBS = 4
SKIPS = (2, 1)
MESH = pl.DeviceIdType.MESH


TAPS = np.arange(-HALF, HALF + 1, dtype=np.float64)
TOTAL = float(np.sum(np.exp(-TAPS * TAPS / (2.0 * SIGMA * SIGMA))))


def band(shape, shift):
    offset = (
        lax.broadcasted_iota(jnp.int32, shape, 1)
        - lax.broadcasted_iota(jnp.int32, shape, 0)
        + shift
    )
    distance = offset.astype(jnp.float32)
    values = jnp.exp(distance * distance * (-1.0 / (2.0 * SIGMA * SIGMA))) * (1.0 / TOTAL)
    return split(jnp.where(jnp.abs(offset) <= HALF, values, jnp.float32(0.0)))


def split(x):
    high = x.astype(jnp.bfloat16)
    low = (x - high.astype(jnp.float32)).astype(jnp.bfloat16)
    return high, low


def dot(a, b):
    return jnp.dot(a, b, preferred_element_type=jnp.float32)


def dot3(a_high, a_low, b_high, b_low):
    return dot(a_high, b_high) + (dot(a_high, b_low) + dot(a_low, b_high))


def kernel(
    sizes,
    rows,
    cols,
    s_hbm,
    d_hbm,
    w_ref,
    raw_ref,
    ku_ref,
    norm_ref,
    brow,
    bedge,
    bcol,
    field,
    dens,
    edge,
    pack,
    strip,
    corner,
    y_high,
    y_low,
    y_edge,
    term,
    sums0,
    sums1,
    asides0,
    asides1,
    m_out,
    m_gx,
    m_gy,
    m_map,
    in_sem,
    halo_send,
    halo_recv,
    sum_sem0,
    sum_sem1,
    aside_sem0,
    aside_sem1,
    all_sem0,
    all_sem1,
    leaf_sem0,
    leaf_sem1,
    m_gx_sem,
    m_gy_sem,
    m_map_sem,
):
    n, ngx, ngy = sizes
    z, gx, gy = lax.axis_index("map"), lax.axis_index("gx"), lax.axis_index("gy")
    main = pl.ds(0, cols)
    quarter = rows // 4
    low_rows, high_rows = pl.ds(0, HALF), pl.ds(rows - HALF, HALF)
    first_tile, last_tile = pl.ds(0, LANES), pl.ds(cols - LANES, LANES)
    halo_tile = pl.ds(cols, LANES)

    load_s = pltpu.make_async_copy(s_hbm.at[0], field.at[0, :, main], in_sem.at[0])
    load_d = pltpu.make_async_copy(d_hbm.at[0], dens, in_sem.at[1])
    load_s.start()
    load_d.start()

    near = []
    for dx in (-1, 0, 1):
        for dy in (-1, 0, 1):
            if dx or dy:
                ok = (gx + dx >= 0) & (gx + dx < ngx) & (gy + dy >= 0) & (gy + dy < ngy)
                near.append((dx, dy, ok))

    barrier = pltpu.get_barrier_semaphore()
    expected = jnp.int32(0)
    for dx, dy, ok in near:
        expected = expected + ok.astype(jnp.int32)

        @pl.when(ok)
        def _():
            pl.semaphore_signal(
                barrier, inc=1, device_id={"gx": gx + dx, "gy": gy + dy}, device_id_type=MESH
            )

    for axis, me, count in (("gx", gx, ngx), ("gy", gy, ngy), ("map", z, n)):
        for k in range(1, count):
            pl.semaphore_signal(
                barrier,
                inc=1,
                device_id={axis: lax.rem(me + k, count)},
                device_id_type=MESH,
            )
        expected = expected + (count - 1)

    def slot(delta):
        return 0 if delta < 0 else 1

    pl.semaphore_wait(barrier, expected)

    def halo_copy(phase, dx, dy):
        if dy == 0:
            source = s_hbm.at[0] if phase == 0 else field.at[1, :, main]
            source = source.at[low_rows if dx < 0 else high_rows]
            target = edge.at[phase, slot(-dx), :, main]
            index = slot(dx)
        elif dx == 0:
            source = pack.at[phase, slot(dy)]
            target = strip.at[phase, slot(-dy)]
            index = 2 + slot(dy)
        else:
            source = field.at[
                phase, low_rows if dx < 0 else high_rows, first_tile if dy < 0 else last_tile
            ]
            target = corner.at[phase, slot(-dx), slot(-dy)]
            index = 4 + 2 * slot(dx) + slot(dy)
        return pltpu.make_async_remote_copy(
            source,
            target,
            halo_send.at[phase, index],
            halo_recv.at[phase, index],
            device_id={"gx": gx + dx, "gy": gy + dy},
            device_id_type=MESH,
        )

    def halo_start(phase, which):
        for dx, dy, ok in near:
            if which(dx, dy):

                @pl.when(ok)
                def _():
                    halo_copy(phase, dx, dy).start()

    lane = lax.broadcasted_iota(jnp.int32, (quarter, LANES), 1)

    def rolled(value, shift):
        return pltpu.roll(value, shift % LANES, 1) if shift % LANES else value

    def pack_strips(phase):
        for q in range(4):
            at = pl.ds(q * quarter, quarter)
            here = (lane >= q * HALF) & (lane < (q + 1) * HALF)
            begin = rolled(field[phase, at, first_tile], q * HALF)
            end = rolled(field[phase, at, last_tile], (q + 1) * HALF)
            if q == 0:
                begin_all, end_all = begin, end
            else:
                begin_all = jnp.where(here, begin, begin_all)
                end_all = jnp.where(here, end, end_all)
        pack[phase, 0] = begin_all
        pack[phase, 1] = end_all

    def joined(left, right, lane):
        zero = jnp.float32(0.0)
        return jnp.where(lane >= LANES - HALF, left, jnp.where(lane < HALF, right, zero))

    def halo_finish(phase):
        for dx, dy, ok in near:
            @pl.when(ok)
            def _():
                halo_copy(phase, -dx, -dy).wait_recv()

        for q in range(4):
            left = rolled(strip[phase, 0], -(q + 1) * HALF)
            right = rolled(strip[phase, 1], -q * HALF)
            field[phase, pl.ds(q * quarter, quarter), halo_tile] = joined(left, right, lane)
        lane_corner = lax.broadcasted_iota(jnp.int32, (HALF, LANES), 1)
        for above in range(2):
            edge[phase, above, :, halo_tile] = joined(
                corner[phase, above, 0], corner[phase, above, 1], lane_corner
            )

    frame = cols + 2 * LANES

    def put(at_rows, at_cols, value):
        y_high[at_rows, at_cols], y_low[at_rows, at_cols] = split(value)

    def row_own(phase):
        def body(block, carry):
            base = pl.multiple_of(block * BLOCK, BLOCK)
            at = pl.ds(base, BLOCK)
            out = dot3(brow[0], brow[1], *split(field[phase, :, at]))
            put(pl.ds(0, rows), pl.ds(pl.multiple_of(base + LANES, LANES), BLOCK), out)
            y_edge[0, :, at] = out[:HALF]
            y_edge[1, :, at] = out[rows - HALF :]
            return carry

        lax.fori_loop(0, cols // BLOCK, body, 0)

    def row_halo(phase):
        out = dot3(brow[0], brow[1], *split(field[phase, :, halo_tile]))
        y_edge[0, :, halo_tile] = out[:HALF]
        y_edge[1, :, halo_tile] = out[rows - HALF :]
        for at in (0, cols + LANES):
            put(pl.ds(0, rows), pl.ds(at, LANES), out)
        for above, at_rows in ((0, low_rows), (1, high_rows)):
            more = dot3(bedge[above, 0], bedge[above, 1], *split(edge[phase, above]))
            total = y_edge[above] + more
            put(at_rows, pl.ds(LANES, cols + LANES), total)
            put(at_rows, pl.ds(0, LANES), total[:, cols:])

    def col_pass(base):
        source = pl.ds(base, 2 * BLOCK)
        return dot3(y_high[:, source], y_low[:, source], bcol[0], bcol[1])

    halo_start(0, lambda dx, dy: dy == 0)
    load_s.wait()
    pack_strips(0)
    halo_start(0, lambda dx, dy: dy != 0)
    for dx, dy, ok in near:

        @pl.when(jnp.logical_not(ok))
        def _():
            for phase in range(2):
                if dy == 0:
                    edge[phase, slot(dx), :, main] = jnp.zeros((HALF, cols), jnp.float32)
                elif dx == 0:
                    strip[phase, slot(dy)] = jnp.zeros((quarter, LANES), jnp.float32)
                else:
                    corner[phase, slot(dx), slot(dy)] = jnp.zeros((HALF, LANES), jnp.float32)

    brow[0], brow[1] = band((rows, rows), 0)
    for above, shift in ((0, -HALF), (1, HALF)):
        bedge[above, 0], bedge[above, 1] = band((HALF, HALF), shift)
    bcol[0], bcol[1] = band((2 * BLOCK, BLOCK), LANES)
    row_own(0)
    halo_finish(0)
    row_halo(0)
    load_d.wait()

    def u_block(block, carry):
        base = pl.multiple_of(block * BLOCK, BLOCK)
        at = pl.ds(base, BLOCK)
        field[1, :, at] = dens[:, at] / col_pass(base)
        return carry

    lax.fori_loop(0, cols // BLOCK, u_block, 0)
    halo_start(1, lambda dx, dy: dy == 0)
    pack_strips(1)
    halo_start(1, lambda dx, dy: dy != 0)
    row_own(1)
    halo_finish(1)
    row_halo(1)
    weight = w_ref[0]

    def ku_block(block, carry):
        base = pl.multiple_of(block * BLOCK, BLOCK)
        at = pl.ds(base, BLOCK)
        ku = col_pass(base)
        ku_ref[:, at] = ku
        term[:, at] = weight * jnp.log(field[0, :, at] * ku)
        return carry

    size = rows // n
    width = cols // SUBS
    hops = (n // 2, (n - 1) // 2)
    skips = SKIPS
    plain = [hops[way] - 2 * skips[way] for way in range(2)]
    steps = [hops[way] - skips[way] for way in range(2)]

    def chunk(d):
        return pl.ds(pl.multiple_of(lax.rem(d + 2 * n, n) * size, 8), size)

    def lanes(sub):
        return pl.ds(sub * width, width)

    def toward(way, sub, distance):
        return z + distance if (sub + way) % 2 == 0 else z - distance

    def device(way, sub, distance):
        return {"map": lax.rem(toward(way, sub, distance) + n, n)}

    sums, asides = (sums0, sums1), (asides0, asides1)
    sum_sems, aside_sems = (sum_sem0, sum_sem1), (aside_sem0, aside_sem1)
    all_sems, leaf_sems = (all_sem0, all_sem1), (leaf_sem0, leaf_sem1)

    def remote(source, target, sems, step, sub, to):
        return pltpu.make_async_remote_copy(
            source,
            target,
            sems.at[0, step, sub],
            sems.at[1, step, sub],
            device_id=to,
            device_id_type=MESH,
        )

    def role(way, step):
        if step < plain[way]:
            return hops[way] - step
        return 2 * (skips[way] - (step - plain[way]))

    def sum_copy(way, step, sub, source=None):
        target = sums[way].at[step, :, lanes(sub)]
        source = target if source is None else source
        to = device(way, sub, 1 if step < plain[way] else 2)
        return remote(source, target, sum_sems[way], step, sub, to)

    def aside_copy(way, index, sub):
        source = term.at[chunk(toward(way, sub, 2 * index + 1)), lanes(sub)]
        target = asides[way].at[index, :, lanes(sub)]
        return remote(source, target, aside_sems[way], index, sub, device(way, sub, 1))

    def arrived(way, step, sub):
        sum_copy(way, step - 1, sub).wait_recv()
        value = sums[way][step - 1, :, lanes(sub)]
        if step > plain[way]:
            index = skips[way] - (step - plain[way])
            aside_copy(way, index, sub).wait_recv()
            value = value + asides[way][index, :, lanes(sub)]
        return value

    def sum_first(sub):
        for way in range(2):
            own = term.at[chunk(toward(way, sub, hops[way])), lanes(sub)]
            sum_copy(way, 0, sub, own).start()

    def sum_next(way, step, sub):
        at = chunk(toward(way, sub, role(way, step)))
        held = sums[way].at[step - 1, :, lanes(sub)]
        held[...] = arrived(way, step, sub) + term[at, lanes(sub)]
        sum_copy(way, step, sub, held).start()

    for block in range(cols // BLOCK):
        ku_block(block, 0)
        for sub in range(SUBS):
            if block * BLOCK < (sub + 1) * width <= (block + 1) * BLOCK:
                sum_first(sub)

    def asides_after(step, sub):
        for way in range(2):
            for index in range(skips[way]):
                use = steps[way] - index
                if step == max(use - 4 + way, 0):
                    aside_copy(way, index, sub).start()

    for sub in range(SUBS):
        asides_after(0, sub)
    for step in range(1, max(steps)):
        for sub in range(SUBS):
            for way in range(2):
                if step < steps[way]:
                    sum_next(way, step, sub)
            asides_after(step, sub)

    def gather_copy(way, step, sub):
        done = 2 * step if step <= skips[way] else step + skips[way]
        ref = raw_ref.at[chunk(toward(way, sub, -done)), lanes(sub)]
        to = device(way, sub, 2 if step < skips[way] else 1)
        return remote(ref, ref, all_sems[way], step, sub, to)

    def leaf_copy(way, index, sub):
        ref = raw_ref.at[chunk(toward(way, sub, -2 * index)), lanes(sub)]
        return remote(ref, ref, leaf_sems[way], index, sub, device(way, sub, 1))

    def gather_start(way, step, sub):
        gather_copy(way, step, sub).start()

    def leaves_after(step, sub):
        for way in range(2):
            for index in range(skips[way]):
                if step == min(2 + index + 2 * way, max(steps) - 2):
                    leaf_copy(way, index, sub).start()

    partial = jnp.zeros((8, LANES), jnp.float32)
    for sub in range(SUBS):
        value = term[chunk(z), lanes(sub)] + arrived(0, steps[0], sub)
        value = jnp.exp(value + arrived(1, steps[1], sub))
        raw_ref[chunk(z), lanes(sub)] = value
        for way in range(2):
            gather_start(way, 0, sub)
        for i in range(size // 8):
            for j in range(width // LANES):
                partial = partial + value[
                    i * 8 : (i + 1) * 8, j * LANES : (j + 1) * LANES
                ]

    def mass_copies(stage, axis, me, count, slots, sems):
        return [
            pltpu.make_async_remote_copy(
                m_out.at[stage],
                slots.at[me],
                sems.at[0, k],
                sems.at[1, me],
                device_id={axis: lax.rem(me + k, count)},
                device_id_type=MESH,
            )
            for k in range(1, count)
        ]

    def mass_start(stage, axis, me, count, slots, sems, value):
        m_out[stage] = value
        slots[me] = value
        for copy in mass_copies(stage, axis, me, count, slots, sems):
            copy.start()

    def mass_finish(stage, axis, me, count, slots, sems):
        for k in range(1, count):
            source = lax.rem(me + k, count)
            pltpu.make_async_remote_copy(
                m_out.at[stage],
                slots.at[source],
                sems.at[0, k],
                sems.at[1, source],
                device_id={axis: source},
                device_id_type=MESH,
            ).wait_recv()
        total = slots[0]
        for i in range(1, count):
            total = total + slots[i]
        return total

    stages = (
        (0, "gx", gx, ngx, m_gx, m_gx_sem),
        (1, "gy", gy, ngy, m_gy, m_gy_sem),
        (2, "map", z, n, m_map, m_map_sem),
    )

    def halos_left():
        for phase in range(2):
            for dx, dy, ok in near:

                @pl.when(ok)
                def _():
                    halo_copy(phase, dx, dy).wait_send()

    def asides_left():
        for sub in range(SUBS):
            for way in range(2):
                for index in range(skips[way]):
                    aside_copy(way, index, sub).wait_send()

    mass_start(*stages[0], partial)
    turns = [1 + (i + 1) * (max(steps) - 1) // 3 for i in range(2)]
    for step in range(1, max(steps) + 1):
        for i in range(2):
            if step == turns[i]:
                total = mass_finish(*stages[i])
                mass_start(*stages[i + 1], total)
                for copy in mass_copies(*stages[i]):
                    copy.wait_send()
        for sub in range(SUBS):
            for way in range(2):
                if step <= steps[way]:
                    gather_copy(way, step - 1, sub).wait_recv()
                if step < steps[way]:
                    gather_start(way, step, sub)
            leaves_after(step, sub)
        if step == 1:
            halos_left()
        if step == 2:
            asides_left()
        for sub in range(SUBS):
            for way in range(2):
                if step - 1 < steps[way]:
                    sum_copy(way, step - 1, sub).wait_send()
                if 2 <= step < steps[way] + 2:
                    gather_copy(way, step - 2, sub).wait_send()
    for sub in range(SUBS):
        for way in range(2):
            for index in range(skips[way]):
                leaf_copy(way, index, sub).wait_recv()

    total = mass_finish(*stages[2])
    cells = float(rows * cols * ngx * ngy)
    norm_ref[...] = jnp.full((1, 1), cells, jnp.float32) / jnp.sum(total)

    for sub in range(SUBS):
        for way in range(2):
            if max(steps) - 1 < steps[way]:
                gather_copy(way, max(steps) - 1, sub).wait_send()
            for index in range(skips[way]):
                leaf_copy(way, index, sub).wait_send()
    for copy in mass_copies(*stages[2]):
        copy.wait_send()


def step(sizes, densities, scaling, weights):
    n, ngx, ngy = sizes
    _, rows, cols = densities.shape
    frame = cols + 2 * LANES
    size = rows // n
    steps = (n // 2 - SKIPS[0], (n - 1) // 2 - SKIPS[1])
    extra = [max(k, 1) for k in SKIPS]
    out = jax.ShapeDtypeStruct((rows, cols), jnp.float32)
    vmem = pl.BlockSpec(memory_space=pltpu.VMEM)
    hbm = pl.BlockSpec(memory_space=pl.ANY)
    dma = pltpu.SemaphoreType.DMA
    f32, bf16 = jnp.float32, jnp.bfloat16
    raw, ku, norm = pl.pallas_call(
        functools.partial(kernel, sizes, rows, cols),
        out_shape=(out, out, jax.ShapeDtypeStruct((1, 1), f32)),
        in_specs=[hbm, hbm, pl.BlockSpec(memory_space=pltpu.SMEM)],
        out_specs=(vmem, vmem, vmem),
        scratch_shapes=[
            pltpu.VMEM((2, rows, rows), bf16),
            pltpu.VMEM((2, 2, HALF, HALF), bf16),
            pltpu.VMEM((2, 2 * BLOCK, BLOCK), bf16),
            pltpu.VMEM((2, rows, cols + LANES), f32),
            pltpu.VMEM((rows, cols), f32),
            pltpu.VMEM((2, 2, HALF, cols + LANES), f32),
            pltpu.VMEM((2, 2, rows // 4, LANES), f32),
            pltpu.VMEM((2, 2, rows // 4, LANES), f32),
            pltpu.VMEM((2, 2, 2, HALF, LANES), f32),
            pltpu.VMEM((rows, frame), bf16),
            pltpu.VMEM((rows, frame), bf16),
            pltpu.VMEM((2, HALF, cols + LANES), f32),
            pltpu.VMEM((rows, cols), f32),
            *[pltpu.VMEM((k, size, cols), f32) for k in (*steps, *extra)],
            pltpu.VMEM((3, 8, LANES), f32),
            pltpu.VMEM((ngx, 8, LANES), f32),
            pltpu.VMEM((ngy, 8, LANES), f32),
            pltpu.VMEM((n, 8, LANES), f32),
            dma((2,)),
            dma((2, 8)),
            dma((2, 8)),
            *[dma((2, k, SUBS)) for k in (*steps, *extra)],
            *[dma((2, k, SUBS)) for k in (*steps, *extra)],
            dma((2, ngx)),
            dma((2, ngy)),
            dma((2, n)),
        ],
        compiler_params=pltpu.CompilerParams(
            collective_id=0, has_side_effects=True, vmem_limit_bytes=50 * 1024 * 1024
        ),
        name="sinkhorn",
    )(scaling, densities, weights)
    barycenter = raw * norm[0, 0]
    new_scaling = barycenter / ku
    return barycenter, new_scaling[None]


def solution(mesh):
    placed = (P("map", "gx", "gy"), P("map", "gx", "gy"), P("map"))
    sizes = (mesh.shape["map"], mesh.shape["gx"], mesh.shape["gy"])
    return jax.shard_map(
        functools.partial(step, sizes),
        mesh=mesh,
        in_specs=placed,
        out_specs=(P("gx", "gy"), P("map", "gx", "gy")),
        check_vma=False,
    )
```

```python
import functools

import jax
import jax.numpy as jnp
import numpy as np
from jax import lax
from jax.experimental import pallas as pl
from jax.experimental.pallas import tpu as pltpu
from jax.sharding import PartitionSpec as P

HALF = 32
SIGMA = 16
LANES = 128
BLOCK = 256
SUBS = 4
SKIPS = (2, 1)
MESH = pl.DeviceIdType.MESH


TAPS = np.arange(-HALF, HALF + 1, dtype=np.float64)
TOTAL = float(np.sum(np.exp(-TAPS * TAPS / (2.0 * SIGMA * SIGMA))))


def band(shape, shift):
    offset = (
        lax.broadcasted_iota(jnp.int32, shape, 1)
        - lax.broadcasted_iota(jnp.int32, shape, 0)
        + shift
    )
    distance = offset.astype(jnp.float32)
    values = jnp.exp(distance * distance * (-1.0 / (2.0 * SIGMA * SIGMA))) * (1.0 / TOTAL)
    return split(jnp.where(jnp.abs(offset) <= HALF, values, jnp.float32(0.0)))


def split(x):
    high = x.astype(jnp.bfloat16)
    low = (x - high.astype(jnp.float32)).astype(jnp.bfloat16)
    return high, low


def dot(a, b):
    return jnp.dot(a, b, preferred_element_type=jnp.float32)


def dot3(a_high, a_low, b_high, b_low):
    return dot(a_high, b_high) + (dot(a_high, b_low) + dot(a_low, b_high))


def kernel(
    sizes,
    rows,
    cols,
    s_hbm,
    d_hbm,
    w_ref,
    raw_ref,
    ku_ref,
    norm_ref,
    brow,
    bedge,
    bcol,
    field,
    dens,
    edge,
    pack,
    strip,
    corner,
    y_high,
    y_low,
    y_edge,
    term,
    sums0,
    sums1,
    asides0,
    asides1,
    m_out,
    m_gx,
    m_gy,
    m_map,
    in_sem,
    halo_send,
    halo_recv,
    sum_sem0,
    sum_sem1,
    aside_sem0,
    aside_sem1,
    all_sem0,
    all_sem1,
    leaf_sem0,
    leaf_sem1,
    m_gx_sem,
    m_gy_sem,
    m_map_sem,
):
    n, ngx, ngy = sizes
    z, gx, gy = lax.axis_index("map"), lax.axis_index("gx"), lax.axis_index("gy")
    main = pl.ds(0, cols)
    quarter = rows // 4
    low_rows, high_rows = pl.ds(0, HALF), pl.ds(rows - HALF, HALF)
    first_tile, last_tile = pl.ds(0, LANES), pl.ds(cols - LANES, LANES)
    halo_tile = pl.ds(cols, LANES)

    load_s = pltpu.make_async_copy(s_hbm.at[0], field.at[0, :, main], in_sem.at[0])
    load_d = pltpu.make_async_copy(d_hbm.at[0], dens, in_sem.at[1])
    load_s.start()
    load_d.start()

    near = []
    for dx in (-1, 0, 1):
        for dy in (-1, 0, 1):
            if dx or dy:
                ok = (gx + dx >= 0) & (gx + dx < ngx) & (gy + dy >= 0) & (gy + dy < ngy)
                near.append((dx, dy, ok))

    barrier = pltpu.get_barrier_semaphore()
    expected = jnp.int32(0)
    for dx, dy, ok in near:
        expected = expected + ok.astype(jnp.int32)

        @pl.when(ok)
        def _():
            pl.semaphore_signal(
                barrier, inc=1, device_id={"gx": gx + dx, "gy": gy + dy}, device_id_type=MESH
            )

    for axis, me, count in (("gx", gx, ngx), ("gy", gy, ngy), ("map", z, n)):
        for k in range(1, count):
            pl.semaphore_signal(
                barrier,
                inc=1,
                device_id={axis: lax.rem(me + k, count)},
                device_id_type=MESH,
            )
        expected = expected + (count - 1)

    def slot(delta):
        return 0 if delta < 0 else 1

    pl.semaphore_wait(barrier, expected)

    def halo_copy(phase, dx, dy, block=0):
        if dy == 0:
            at_rows = low_rows if dx < 0 else high_rows
            at = pl.ds(block * BLOCK, BLOCK)
            source = s_hbm.at[0, at_rows, at] if phase == 0 else field.at[1, at_rows, at]
            target = edge.at[phase, slot(-dx), :, at]
            index = 6 + 2 * block + slot(dx)
        elif dx == 0:
            source = pack.at[phase, slot(dy)]
            target = strip.at[phase, slot(-dy)]
            index = slot(dy)
        else:
            source = field.at[
                phase, low_rows if dx < 0 else high_rows, first_tile if dy < 0 else last_tile
            ]
            target = corner.at[phase, slot(-dx), slot(-dy)]
            index = 2 + 2 * slot(dx) + slot(dy)
        return pltpu.make_async_remote_copy(
            source,
            target,
            halo_send.at[phase, index],
            halo_recv.at[phase, index],
            device_id={"gx": gx + dx, "gy": gy + dy},
            device_id_type=MESH,
        )

    def pieces(dy):
        return range(cols // BLOCK) if dy == 0 else range(1)

    def rows_start(phase, block):
        for dx, dy, ok in near:
            if dy == 0:

                @pl.when(ok)
                def _():
                    halo_copy(phase, dx, dy, block).start()

    def sides_start(phase):
        for dx, dy, ok in near:
            if dy != 0:

                @pl.when(ok)
                def _():
                    halo_copy(phase, dx, dy).start()

    lane = lax.broadcasted_iota(jnp.int32, (quarter, LANES), 1)

    def rolled(value, shift):
        return pltpu.roll(value, shift % LANES, 1) if shift % LANES else value

    def pack_strips(phase):
        for q in range(4):
            at = pl.ds(q * quarter, quarter)
            here = (lane >= q * HALF) & (lane < (q + 1) * HALF)
            begin = rolled(field[phase, at, first_tile], q * HALF)
            end = rolled(field[phase, at, last_tile], (q + 1) * HALF)
            if q == 0:
                begin_all, end_all = begin, end
            else:
                begin_all = jnp.where(here, begin, begin_all)
                end_all = jnp.where(here, end, end_all)
        pack[phase, 0] = begin_all
        pack[phase, 1] = end_all

    def joined(left, right, lane):
        zero = jnp.float32(0.0)
        return jnp.where(lane >= LANES - HALF, left, jnp.where(lane < HALF, right, zero))

    def halo_finish(phase):
        for dx, dy, ok in near:
            @pl.when(ok)
            def _():
                for block in pieces(dy):
                    halo_copy(phase, -dx, -dy, block).wait_recv()

        for q in range(4):
            left = rolled(strip[phase, 0], -(q + 1) * HALF)
            right = rolled(strip[phase, 1], -q * HALF)
            field[phase, pl.ds(q * quarter, quarter), halo_tile] = joined(left, right, lane)
        lane_corner = lax.broadcasted_iota(jnp.int32, (HALF, LANES), 1)
        for above in range(2):
            edge[phase, above, :, halo_tile] = joined(
                corner[phase, above, 0], corner[phase, above, 1], lane_corner
            )

    frame = cols + 2 * LANES

    def put(at_rows, at_cols, value):
        y_high[at_rows, at_cols], y_low[at_rows, at_cols] = split(value)

    def row_own(phase):
        def body(block, carry):
            base = pl.multiple_of(block * BLOCK, BLOCK)
            at = pl.ds(base, BLOCK)
            out = dot3(brow[0], brow[1], *split(field[phase, :, at]))
            put(pl.ds(0, rows), pl.ds(pl.multiple_of(base + LANES, LANES), BLOCK), out)
            y_edge[0, :, at] = out[:HALF]
            y_edge[1, :, at] = out[rows - HALF :]
            return carry

        lax.fori_loop(0, cols // BLOCK, body, 0)

    def row_halo(phase):
        out = dot3(brow[0], brow[1], *split(field[phase, :, halo_tile]))
        y_edge[0, :, halo_tile] = out[:HALF]
        y_edge[1, :, halo_tile] = out[rows - HALF :]
        for at in (0, cols + LANES):
            put(pl.ds(0, rows), pl.ds(at, LANES), out)
        for above, at_rows in ((0, low_rows), (1, high_rows)):
            more = dot3(bedge[above, 0], bedge[above, 1], *split(edge[phase, above]))
            total = y_edge[above] + more
            put(at_rows, pl.ds(LANES, cols + LANES), total)
            put(at_rows, pl.ds(0, LANES), total[:, cols:])

    def col_pass(base):
        source = pl.ds(base, 2 * BLOCK)
        return dot3(y_high[:, source], y_low[:, source], bcol[0], bcol[1])

    for block in pieces(0):
        rows_start(0, block)
    load_s.wait()
    pack_strips(0)
    sides_start(0)
    for dx, dy, ok in near:

        @pl.when(jnp.logical_not(ok))
        def _():
            for phase in range(2):
                if dy == 0:
                    edge[phase, slot(dx), :, main] = jnp.zeros((HALF, cols), jnp.float32)
                elif dx == 0:
                    strip[phase, slot(dy)] = jnp.zeros((quarter, LANES), jnp.float32)
                else:
                    corner[phase, slot(dx), slot(dy)] = jnp.zeros((HALF, LANES), jnp.float32)

    brow[0], brow[1] = band((rows, rows), 0)
    for above, shift in ((0, -HALF), (1, HALF)):
        bedge[above, 0], bedge[above, 1] = band((HALF, HALF), shift)
    bcol[0], bcol[1] = band((2 * BLOCK, BLOCK), LANES)
    row_own(0)
    halo_finish(0)
    row_halo(0)
    load_d.wait()

    def u_block(block, carry):
        base = pl.multiple_of(block * BLOCK, BLOCK)
        at = pl.ds(base, BLOCK)
        field[1, :, at] = dens[:, at] / col_pass(base)
        return carry

    outer = list(dict.fromkeys((0, cols // BLOCK - 1)))
    for block in outer:
        u_block(block, 0)
        rows_start(1, block)
    pack_strips(1)
    sides_start(1)
    for block in range(1, cols // BLOCK - 1):
        u_block(block, 0)
        rows_start(1, block)
    row_own(1)
    halo_finish(1)
    row_halo(1)
    weight = w_ref[0]

    def ku_block(block, carry):
        base = pl.multiple_of(block * BLOCK, BLOCK)
        at = pl.ds(base, BLOCK)
        ku = col_pass(base)
        ku_ref[:, at] = ku
        term[:, at] = weight * jnp.log(field[0, :, at] * ku)
        return carry

    size = rows // n
    width = cols // SUBS
    hops = (n // 2, (n - 1) // 2)
    skips = SKIPS
    plain = [hops[way] - 2 * skips[way] for way in range(2)]
    steps = [hops[way] - skips[way] for way in range(2)]

    def chunk(d):
        return pl.ds(pl.multiple_of(lax.rem(d + 2 * n, n) * size, 8), size)

    def lanes(sub):
        return pl.ds(sub * width, width)

    def toward(way, sub, distance):
        return z + distance if (sub + way) % 2 == 0 else z - distance

    def device(way, sub, distance):
        return {"map": lax.rem(toward(way, sub, distance) + n, n)}

    sums, asides = (sums0, sums1), (asides0, asides1)
    sum_sems, aside_sems = (sum_sem0, sum_sem1), (aside_sem0, aside_sem1)
    all_sems, leaf_sems = (all_sem0, all_sem1), (leaf_sem0, leaf_sem1)

    def remote(source, target, sems, step, sub, to):
        return pltpu.make_async_remote_copy(
            source,
            target,
            sems.at[0, step, sub],
            sems.at[1, step, sub],
            device_id=to,
            device_id_type=MESH,
        )

    def role(way, step):
        if step < plain[way]:
            return hops[way] - step
        return 2 * (skips[way] - (step - plain[way]))

    def sum_copy(way, step, sub, source=None):
        target = sums[way].at[step, :, lanes(sub)]
        source = target if source is None else source
        to = device(way, sub, 1 if step < plain[way] else 2)
        return remote(source, target, sum_sems[way], step, sub, to)

    def aside_copy(way, index, sub):
        source = term.at[chunk(toward(way, sub, 2 * index + 1)), lanes(sub)]
        target = asides[way].at[index, :, lanes(sub)]
        return remote(source, target, aside_sems[way], index, sub, device(way, sub, 1))

    def arrived(way, step, sub):
        sum_copy(way, step - 1, sub).wait_recv()
        value = sums[way][step - 1, :, lanes(sub)]
        if step > plain[way]:
            index = skips[way] - (step - plain[way])
            aside_copy(way, index, sub).wait_recv()
            value = value + asides[way][index, :, lanes(sub)]
        return value

    def sum_first(sub):
        for way in range(2):
            own = term.at[chunk(toward(way, sub, hops[way])), lanes(sub)]
            sum_copy(way, 0, sub, own).start()

    def sum_next(way, step, sub):
        at = chunk(toward(way, sub, role(way, step)))
        held = sums[way].at[step - 1, :, lanes(sub)]
        held[...] = arrived(way, step, sub) + term[at, lanes(sub)]
        sum_copy(way, step, sub, held).start()

    for block in range(cols // BLOCK):
        ku_block(block, 0)
        for sub in range(SUBS):
            if block * BLOCK < (sub + 1) * width <= (block + 1) * BLOCK:
                sum_first(sub)

    def asides_after(step, sub):
        for way in range(2):
            for index in range(skips[way]):
                use = steps[way] - index
                if step == max(use - 4 + way, 0):
                    aside_copy(way, index, sub).start()

    for sub in range(SUBS):
        asides_after(0, sub)
    for step in range(1, max(steps)):
        for sub in range(SUBS):
            for way in range(2):
                if step < steps[way]:
                    sum_next(way, step, sub)
            asides_after(step, sub)

    def gather_copy(way, step, sub):
        done = 2 * step if step <= skips[way] else step + skips[way]
        ref = raw_ref.at[chunk(toward(way, sub, -done)), lanes(sub)]
        to = device(way, sub, 2 if step < skips[way] else 1)
        return remote(ref, ref, all_sems[way], step, sub, to)

    def leaf_copy(way, index, sub):
        ref = raw_ref.at[chunk(toward(way, sub, -2 * index)), lanes(sub)]
        return remote(ref, ref, leaf_sems[way], index, sub, device(way, sub, 1))

    def gather_start(way, step, sub):
        gather_copy(way, step, sub).start()

    def leaves_after(step, sub):
        for way in range(2):
            for index in range(skips[way]):
                if step == min(2 + index + 2 * way, max(steps) - 2):
                    leaf_copy(way, index, sub).start()

    partial = jnp.zeros((8, LANES), jnp.float32)
    for sub in range(SUBS):
        value = term[chunk(z), lanes(sub)] + arrived(0, steps[0], sub)
        value = jnp.exp(value + arrived(1, steps[1], sub))
        raw_ref[chunk(z), lanes(sub)] = value
        for way in range(2):
            gather_start(way, 0, sub)
        for i in range(size // 8):
            for j in range(width // LANES):
                partial = partial + value[
                    i * 8 : (i + 1) * 8, j * LANES : (j + 1) * LANES
                ]

    def mass_copies(stage, axis, me, count, slots, sems):
        return [
            pltpu.make_async_remote_copy(
                m_out.at[stage],
                slots.at[me],
                sems.at[0, k],
                sems.at[1, me],
                device_id={axis: lax.rem(me + k, count)},
                device_id_type=MESH,
            )
            for k in range(1, count)
        ]

    def mass_start(stage, axis, me, count, slots, sems, value):
        m_out[stage] = value
        slots[me] = value
        for copy in mass_copies(stage, axis, me, count, slots, sems):
            copy.start()

    def mass_finish(stage, axis, me, count, slots, sems):
        for k in range(1, count):
            source = lax.rem(me + k, count)
            pltpu.make_async_remote_copy(
                m_out.at[stage],
                slots.at[source],
                sems.at[0, k],
                sems.at[1, source],
                device_id={axis: source},
                device_id_type=MESH,
            ).wait_recv()
        total = slots[0]
        for i in range(1, count):
            total = total + slots[i]
        return total

    stages = (
        (0, "gx", gx, ngx, m_gx, m_gx_sem),
        (1, "gy", gy, ngy, m_gy, m_gy_sem),
        (2, "map", z, n, m_map, m_map_sem),
    )

    def halos_left():
        for phase in range(2):
            for dx, dy, ok in near:

                @pl.when(ok)
                def _():
                    for block in pieces(dy):
                        halo_copy(phase, dx, dy, block).wait_send()

    def asides_left():
        for sub in range(SUBS):
            for way in range(2):
                for index in range(skips[way]):
                    aside_copy(way, index, sub).wait_send()

    mass_start(*stages[0], partial)
    turns = [1 + (i + 1) * (max(steps) - 1) // 3 for i in range(2)]
    for step in range(1, max(steps) + 1):
        for i in range(2):
            if step == turns[i]:
                total = mass_finish(*stages[i])
                mass_start(*stages[i + 1], total)
                for copy in mass_copies(*stages[i]):
                    copy.wait_send()
        for sub in range(SUBS):
            for way in range(2):
                if step <= steps[way]:
                    gather_copy(way, step - 1, sub).wait_recv()
                if step < steps[way]:
                    gather_start(way, step, sub)
            leaves_after(step, sub)
        if step == 1:
            halos_left()
        if step == 2:
            asides_left()
        for sub in range(SUBS):
            for way in range(2):
                if step - 1 < steps[way]:
                    sum_copy(way, step - 1, sub).wait_send()
                if 2 <= step < steps[way] + 2:
                    gather_copy(way, step - 2, sub).wait_send()
    for sub in range(SUBS):
        for way in range(2):
            for index in range(skips[way]):
                leaf_copy(way, index, sub).wait_recv()

    total = mass_finish(*stages[2])
    cells = float(rows * cols * ngx * ngy)
    norm_ref[...] = jnp.full((1, 1), cells, jnp.float32) / jnp.sum(total)

    for sub in range(SUBS):
        for way in range(2):
            if max(steps) - 1 < steps[way]:
                gather_copy(way, max(steps) - 1, sub).wait_send()
            for index in range(skips[way]):
                leaf_copy(way, index, sub).wait_send()
    for copy in mass_copies(*stages[2]):
        copy.wait_send()


def step(sizes, densities, scaling, weights):
    n, ngx, ngy = sizes
    _, rows, cols = densities.shape
    frame = cols + 2 * LANES
    size = rows // n
    steps = (n // 2 - SKIPS[0], (n - 1) // 2 - SKIPS[1])
    extra = [max(k, 1) for k in SKIPS]
    out = jax.ShapeDtypeStruct((rows, cols), jnp.float32)
    vmem = pl.BlockSpec(memory_space=pltpu.VMEM)
    hbm = pl.BlockSpec(memory_space=pl.ANY)
    dma = pltpu.SemaphoreType.DMA
    f32, bf16 = jnp.float32, jnp.bfloat16
    raw, ku, norm = pl.pallas_call(
        functools.partial(kernel, sizes, rows, cols),
        out_shape=(out, out, jax.ShapeDtypeStruct((1, 1), f32)),
        in_specs=[hbm, hbm, pl.BlockSpec(memory_space=pltpu.SMEM)],
        out_specs=(vmem, vmem, vmem),
        scratch_shapes=[
            pltpu.VMEM((2, rows, rows), bf16),
            pltpu.VMEM((2, 2, HALF, HALF), bf16),
            pltpu.VMEM((2, 2 * BLOCK, BLOCK), bf16),
            pltpu.VMEM((2, rows, cols + LANES), f32),
            pltpu.VMEM((rows, cols), f32),
            pltpu.VMEM((2, 2, HALF, cols + LANES), f32),
            pltpu.VMEM((2, 2, rows // 4, LANES), f32),
            pltpu.VMEM((2, 2, rows // 4, LANES), f32),
            pltpu.VMEM((2, 2, 2, HALF, LANES), f32),
            pltpu.VMEM((rows, frame), bf16),
            pltpu.VMEM((rows, frame), bf16),
            pltpu.VMEM((2, HALF, cols + LANES), f32),
            pltpu.VMEM((rows, cols), f32),
            *[pltpu.VMEM((k, size, cols), f32) for k in (*steps, *extra)],
            pltpu.VMEM((3, 8, LANES), f32),
            pltpu.VMEM((ngx, 8, LANES), f32),
            pltpu.VMEM((ngy, 8, LANES), f32),
            pltpu.VMEM((n, 8, LANES), f32),
            dma((2,)),
            dma((2, 6 + 2 * (cols // BLOCK))),
            dma((2, 6 + 2 * (cols // BLOCK))),
            *[dma((2, k, SUBS)) for k in (*steps, *extra)],
            *[dma((2, k, SUBS)) for k in (*steps, *extra)],
            dma((2, ngx)),
            dma((2, ngy)),
            dma((2, n)),
        ],
        compiler_params=pltpu.CompilerParams(
            collective_id=0, has_side_effects=True, vmem_limit_bytes=50 * 1024 * 1024
        ),
        name="sinkhorn",
    )(scaling, densities, weights)
    barycenter = raw * norm[0, 0]
    new_scaling = barycenter / ku
    return barycenter, new_scaling[None]


def solution(mesh):
    placed = (P("map", "gx", "gy"), P("map", "gx", "gy"), P("map"))
    sizes = (mesh.shape["map"], mesh.shape["gx"], mesh.shape["gy"])
    return jax.shard_map(
        functools.partial(step, sizes),
        mesh=mesh,
        in_specs=placed,
        out_specs=(P("gx", "gy"), P("map", "gx", "gy")),
        check_vma=False,
    )
```

```python
import functools

import jax
import jax.numpy as jnp
import numpy as np
from jax import lax
from jax.experimental import pallas as pl
from jax.experimental.pallas import tpu as pltpu
from jax.sharding import PartitionSpec as P

HALF = 32
SIGMA = 16
LANES = 128
BLOCK = 256
SUBS = 4
SKIPS = (2, 1)
MESH = pl.DeviceIdType.MESH


TAPS = np.arange(-HALF, HALF + 1, dtype=np.float64)
TOTAL = float(np.sum(np.exp(-TAPS * TAPS / (2.0 * SIGMA * SIGMA))))


def band(shape, shift):
    offset = (
        lax.broadcasted_iota(jnp.int32, shape, 1)
        - lax.broadcasted_iota(jnp.int32, shape, 0)
        + shift
    )
    distance = offset.astype(jnp.float32)
    values = jnp.exp(distance * distance * (-1.0 / (2.0 * SIGMA * SIGMA))) * (1.0 / TOTAL)
    return split(jnp.where(jnp.abs(offset) <= HALF, values, jnp.float32(0.0)))


def split(x):
    high = x.astype(jnp.bfloat16)
    low = (x - high.astype(jnp.float32)).astype(jnp.bfloat16)
    return high, low


def dot(a, b):
    return jnp.dot(a, b, preferred_element_type=jnp.float32)


def dot3(a_high, a_low, b_high, b_low):
    return dot(a_high, b_high) + (dot(a_high, b_low) + dot(a_low, b_high))


def kernel(
    sizes,
    rows,
    cols,
    s_hbm,
    d_hbm,
    w_ref,
    raw_ref,
    ku_ref,
    norm_ref,
    brow,
    bedge,
    bcol,
    field,
    dens,
    edge,
    pack,
    strip,
    corner,
    y_high,
    y_low,
    y_edge,
    term,
    sums0,
    sums1,
    asides0,
    asides1,
    m_out,
    m_gx,
    m_gy,
    m_map,
    in_sem,
    halo_send,
    halo_recv,
    sum_sem0,
    sum_sem1,
    aside_sem0,
    aside_sem1,
    all_sem0,
    all_sem1,
    leaf_sem0,
    leaf_sem1,
    m_gx_sem,
    m_gy_sem,
    m_map_sem,
):
    n, ngx, ngy = sizes
    z, gx, gy = lax.axis_index("map"), lax.axis_index("gx"), lax.axis_index("gy")
    main = pl.ds(0, cols)
    quarter = rows // 4
    low_rows, high_rows = pl.ds(0, HALF), pl.ds(rows - HALF, HALF)
    first_tile, last_tile = pl.ds(0, LANES), pl.ds(cols - LANES, LANES)
    halo_tile = pl.ds(cols, LANES)

    load_s = pltpu.make_async_copy(s_hbm.at[0], field.at[0, :, main], in_sem.at[0])
    load_d = pltpu.make_async_copy(d_hbm.at[0], dens, in_sem.at[1])
    load_s.start()
    load_d.start()

    near = []
    for dx in (-1, 0, 1):
        for dy in (-1, 0, 1):
            if dx or dy:
                ok = (gx + dx >= 0) & (gx + dx < ngx) & (gy + dy >= 0) & (gy + dy < ngy)
                near.append((dx, dy, ok))

    barrier = pltpu.get_barrier_semaphore()
    expected = jnp.int32(0)
    for dx, dy, ok in near:
        expected = expected + ok.astype(jnp.int32)

        @pl.when(ok)
        def _():
            pl.semaphore_signal(
                barrier, inc=1, device_id={"gx": gx + dx, "gy": gy + dy}, device_id_type=MESH
            )

    for axis, me, count in (("gx", gx, ngx), ("gy", gy, ngy), ("map", z, n)):
        for k in range(1, count):
            pl.semaphore_signal(
                barrier,
                inc=1,
                device_id={axis: lax.rem(me + k, count)},
                device_id_type=MESH,
            )
        expected = expected + (count - 1)

    def slot(delta):
        return 0 if delta < 0 else 1

    pl.semaphore_wait(barrier, expected)

    def halo_copy(phase, dx, dy, block=0):
        if dy == 0:
            at_rows = low_rows if dx < 0 else high_rows
            at = pl.ds(block * BLOCK, BLOCK)
            source = s_hbm.at[0, at_rows, at] if phase == 0 else field.at[1, at_rows, at]
            target = edge.at[phase, slot(-dx), :, at]
            index = 6 + 2 * block + slot(dx)
        elif dx == 0:
            source = pack.at[phase, slot(dy)]
            target = strip.at[phase, slot(-dy)]
            index = slot(dy)
        else:
            source = field.at[
                phase, low_rows if dx < 0 else high_rows, first_tile if dy < 0 else last_tile
            ]
            target = corner.at[phase, slot(-dx), slot(-dy)]
            index = 2 + 2 * slot(dx) + slot(dy)
        return pltpu.make_async_remote_copy(
            source,
            target,
            halo_send.at[phase, index],
            halo_recv.at[phase, index],
            device_id={"gx": gx + dx, "gy": gy + dy},
            device_id_type=MESH,
        )

    def pieces(dy):
        return range(cols // BLOCK) if dy == 0 else range(1)

    def rows_start(phase, block):
        for dx, dy, ok in near:
            if dy == 0:

                @pl.when(ok)
                def _():
                    halo_copy(phase, dx, dy, block).start()

    def sides_start(phase):
        for dx, dy, ok in near:
            if dy != 0:

                @pl.when(ok)
                def _():
                    halo_copy(phase, dx, dy).start()

    lane = lax.broadcasted_iota(jnp.int32, (quarter, LANES), 1)

    def rolled(value, shift):
        return pltpu.roll(value, shift % LANES, 1) if shift % LANES else value

    def pack_strips(phase):
        for q in range(4):
            at = pl.ds(q * quarter, quarter)
            here = (lane >= q * HALF) & (lane < (q + 1) * HALF)
            begin = rolled(field[phase, at, first_tile], q * HALF)
            end = rolled(field[phase, at, last_tile], (q + 1) * HALF)
            if q == 0:
                begin_all, end_all = begin, end
            else:
                begin_all = jnp.where(here, begin, begin_all)
                end_all = jnp.where(here, end, end_all)
        pack[phase, 0] = begin_all
        pack[phase, 1] = end_all

    def joined(left, right, lane):
        zero = jnp.float32(0.0)
        return jnp.where(lane >= LANES - HALF, left, jnp.where(lane < HALF, right, zero))

    def halo_finish(phase):
        for dx, dy, ok in near:
            @pl.when(ok)
            def _():
                for block in pieces(dy):
                    halo_copy(phase, -dx, -dy, block).wait_recv()

        for q in range(4):
            left = rolled(strip[phase, 0], -(q + 1) * HALF)
            right = rolled(strip[phase, 1], -q * HALF)
            field[phase, pl.ds(q * quarter, quarter), halo_tile] = joined(left, right, lane)
        lane_corner = lax.broadcasted_iota(jnp.int32, (HALF, LANES), 1)
        for above in range(2):
            edge[phase, above, :, halo_tile] = joined(
                corner[phase, above, 0], corner[phase, above, 1], lane_corner
            )

    frame = cols + 2 * LANES

    def put(at_rows, at_cols, value):
        y_high[at_rows, at_cols], y_low[at_rows, at_cols] = split(value)

    def row_own(phase):
        def body(block, carry):
            base = pl.multiple_of(block * BLOCK, BLOCK)
            at = pl.ds(base, BLOCK)
            out = dot3(brow[0], brow[1], *split(field[phase, :, at]))
            put(pl.ds(0, rows), pl.ds(pl.multiple_of(base + LANES, LANES), BLOCK), out)
            y_edge[0, :, at] = out[:HALF]
            y_edge[1, :, at] = out[rows - HALF :]
            return carry

        lax.fori_loop(0, cols // BLOCK, body, 0)

    def row_halo(phase):
        out = dot3(brow[0], brow[1], *split(field[phase, :, halo_tile]))
        y_edge[0, :, halo_tile] = out[:HALF]
        y_edge[1, :, halo_tile] = out[rows - HALF :]
        for at in (0, cols + LANES):
            put(pl.ds(0, rows), pl.ds(at, LANES), out)
        for above, at_rows in ((0, low_rows), (1, high_rows)):
            more = dot3(bedge[above, 0], bedge[above, 1], *split(edge[phase, above]))
            total = y_edge[above] + more
            put(at_rows, pl.ds(LANES, cols + LANES), total)
            put(at_rows, pl.ds(0, LANES), total[:, cols:])

    def col_pass(base):
        source = pl.ds(base, 2 * BLOCK)
        return dot3(y_high[:, source], y_low[:, source], bcol[0], bcol[1])

    for block in pieces(0):
        rows_start(0, block)
    load_s.wait()
    pack_strips(0)
    sides_start(0)
    for dx, dy, ok in near:

        @pl.when(jnp.logical_not(ok))
        def _():
            for phase in range(2):
                if dy == 0:
                    edge[phase, slot(dx), :, main] = jnp.zeros((HALF, cols), jnp.float32)
                elif dx == 0:
                    strip[phase, slot(dy)] = jnp.zeros((quarter, LANES), jnp.float32)
                else:
                    corner[phase, slot(dx), slot(dy)] = jnp.zeros((HALF, LANES), jnp.float32)

    brow[0], brow[1] = band((rows, rows), 0)
    for above, shift in ((0, -HALF), (1, HALF)):
        bedge[above, 0], bedge[above, 1] = band((HALF, HALF), shift)
    bcol[0], bcol[1] = band((2 * BLOCK, BLOCK), LANES)
    row_own(0)
    halo_finish(0)
    row_halo(0)
    load_d.wait()

    def u_block(block, carry):
        base = pl.multiple_of(block * BLOCK, BLOCK)
        at = pl.ds(base, BLOCK)
        field[1, :, at] = dens[:, at] / col_pass(base)
        return carry

    outer = list(dict.fromkeys((0, cols // BLOCK - 1)))
    for block in outer:
        u_block(block, 0)
        rows_start(1, block)
    pack_strips(1)
    sides_start(1)
    for block in range(1, cols // BLOCK - 1):
        u_block(block, 0)
        rows_start(1, block)
    row_own(1)
    halo_finish(1)
    row_halo(1)
    weight = w_ref[0]

    def ku_block(block, carry):
        base = pl.multiple_of(block * BLOCK, BLOCK)
        at = pl.ds(base, BLOCK)
        ku = col_pass(base)
        ku_ref[:, at] = ku
        term[:, at] = weight * jnp.log(field[0, :, at] * ku)
        return carry

    size = rows // n
    width = cols // SUBS
    hops = (n // 2, (n - 1) // 2)
    skips = SKIPS
    plain = [hops[way] - 2 * skips[way] for way in range(2)]
    steps = [hops[way] - skips[way] for way in range(2)]

    def chunk(d):
        return pl.ds(pl.multiple_of(lax.rem(d + 2 * n, n) * size, 8), size)

    def lanes(sub):
        return pl.ds(sub * width, width)

    def toward(way, sub, distance):
        return z + distance if (sub + way) % 2 == 0 else z - distance

    def device(way, sub, distance):
        return {"map": lax.rem(toward(way, sub, distance) + n, n)}

    sums, asides = (sums0, sums1), (asides0, asides1)
    sum_sems, aside_sems = (sum_sem0, sum_sem1), (aside_sem0, aside_sem1)
    all_sems, leaf_sems = (all_sem0, all_sem1), (leaf_sem0, leaf_sem1)

    def remote(source, target, sems, step, sub, to):
        return pltpu.make_async_remote_copy(
            source,
            target,
            sems.at[0, step, sub],
            sems.at[1, step, sub],
            device_id=to,
            device_id_type=MESH,
        )

    def role(way, step):
        if step < plain[way]:
            return hops[way] - step
        return 2 * (skips[way] - (step - plain[way]))

    def sum_copy(way, step, sub, source=None):
        target = sums[way].at[step, :, lanes(sub)]
        source = target if source is None else source
        to = device(way, sub, 1 if step < plain[way] else 2)
        return remote(source, target, sum_sems[way], step, sub, to)

    def aside_copy(way, index, sub):
        source = term.at[chunk(toward(way, sub, 2 * index + 1)), lanes(sub)]
        target = asides[way].at[index, :, lanes(sub)]
        return remote(source, target, aside_sems[way], index, sub, device(way, sub, 1))

    def arrived(way, step, sub):
        sum_copy(way, step - 1, sub).wait_recv()
        value = sums[way][step - 1, :, lanes(sub)]
        if step > plain[way]:
            index = skips[way] - (step - plain[way])
            aside_copy(way, index, sub).wait_recv()
            value = value + asides[way][index, :, lanes(sub)]
        return value

    def sum_first(sub):
        for way in range(2):
            own = term.at[chunk(toward(way, sub, hops[way])), lanes(sub)]
            sum_copy(way, 0, sub, own).start()

    def sum_next(way, step, sub):
        at = chunk(toward(way, sub, role(way, step)))
        held = sums[way].at[step - 1, :, lanes(sub)]
        held[...] = arrived(way, step, sub) + term[at, lanes(sub)]
        sum_copy(way, step, sub, held).start()

    for block in range(cols // BLOCK):
        ku_block(block, 0)
        for sub in range(SUBS):
            if block * BLOCK < (sub + 1) * width <= (block + 1) * BLOCK:
                sum_first(sub)

    def asides_after(step, sub):
        for way in range(2):
            for index in range(skips[way]):
                use = steps[way] - index
                if step == max(use - 4 + way, 0):
                    aside_copy(way, index, sub).start()

    for sub in range(SUBS):
        asides_after(0, sub)
    for step in range(1, max(steps)):
        for sub in range(SUBS):
            for way in range(2):
                if step < steps[way]:
                    sum_next(way, step, sub)
            asides_after(step, sub)

    def gather_copy(way, step, sub):
        done = 2 * step if step <= skips[way] else step + skips[way]
        ref = raw_ref.at[chunk(toward(way, sub, -done)), lanes(sub)]
        to = device(way, sub, 2 if step < skips[way] else 1)
        return remote(ref, ref, all_sems[way], step, sub, to)

    def leaf_copy(way, index, sub):
        ref = raw_ref.at[chunk(toward(way, sub, -2 * index)), lanes(sub)]
        return remote(ref, ref, leaf_sems[way], index, sub, device(way, sub, 1))

    def gather_start(way, step, sub):
        gather_copy(way, step, sub).start()

    def leaves_after(step, sub):
        for way in range(2):
            for index in range(skips[way]):
                if step == min(2 + index + 2 * way, max(steps) - 2):
                    leaf_copy(way, index, sub).start()

    partial = jnp.zeros((8, LANES), jnp.float32)
    for sub in range(SUBS):
        value = term[chunk(z), lanes(sub)] + arrived(0, steps[0], sub)
        value = jnp.exp(value + arrived(1, steps[1], sub))
        raw_ref[chunk(z), lanes(sub)] = value
        for way in range(2):
            gather_start(way, 0, sub)
        for i in range(size // 8):
            for j in range(width // LANES):
                partial = partial + value[
                    i * 8 : (i + 1) * 8, j * LANES : (j + 1) * LANES
                ]

    def mass_copies(stage, axis, me, count, slots, sems):
        return [
            pltpu.make_async_remote_copy(
                m_out.at[stage],
                slots.at[me],
                sems.at[0, k],
                sems.at[1, me],
                device_id={axis: lax.rem(me + k, count)},
                device_id_type=MESH,
            )
            for k in range(1, count)
        ]

    def mass_start(stage, axis, me, count, slots, sems, value):
        m_out[stage] = value
        slots[me] = value
        for copy in mass_copies(stage, axis, me, count, slots, sems):
            copy.start()

    def mass_finish(stage, axis, me, count, slots, sems):
        for k in range(1, count):
            source = lax.rem(me + k, count)
            pltpu.make_async_remote_copy(
                m_out.at[stage],
                slots.at[source],
                sems.at[0, k],
                sems.at[1, source],
                device_id={axis: source},
                device_id_type=MESH,
            ).wait_recv()
        total = slots[0]
        for i in range(1, count):
            total = total + slots[i]
        return total

    stages = (
        (0, "gx", gx, ngx, m_gx, m_gx_sem),
        (1, "gy", gy, ngy, m_gy, m_gy_sem),
        (2, "map", z, n, m_map, m_map_sem),
    )

    def halos_left():
        for phase in range(2):
            for dx, dy, ok in near:

                @pl.when(ok)
                def _():
                    for block in pieces(dy):
                        halo_copy(phase, dx, dy, block).wait_send()

    def asides_left():
        for sub in range(SUBS):
            for way in range(2):
                for index in range(skips[way]):
                    aside_copy(way, index, sub).wait_send()

    mass_start(*stages[0], partial)
    turns = [max(max(steps) - 3 + 2 * i, 1) for i in range(2)]
    for step in range(1, max(steps) + 1):
        for i in range(2):
            if step == turns[i]:
                total = mass_finish(*stages[i])
                mass_start(*stages[i + 1], total)
                for copy in mass_copies(*stages[i]):
                    copy.wait_send()
        for sub in range(SUBS):
            for way in range(2):
                if step <= steps[way]:
                    gather_copy(way, step - 1, sub).wait_recv()
                if step < steps[way]:
                    gather_start(way, step, sub)
            leaves_after(step, sub)
        if step == 1:
            halos_left()
        if step == 2:
            asides_left()
        for sub in range(SUBS):
            for way in range(2):
                if step - 1 < steps[way]:
                    sum_copy(way, step - 1, sub).wait_send()
                if 2 <= step < steps[way] + 2:
                    gather_copy(way, step - 2, sub).wait_send()
    for sub in range(SUBS):
        for way in range(2):
            for index in range(skips[way]):
                leaf_copy(way, index, sub).wait_recv()

    total = mass_finish(*stages[2])
    cells = float(rows * cols * ngx * ngy)
    norm_ref[...] = jnp.full((1, 1), cells, jnp.float32) / jnp.sum(total)

    for sub in range(SUBS):
        for way in range(2):
            if max(steps) - 1 < steps[way]:
                gather_copy(way, max(steps) - 1, sub).wait_send()
            for index in range(skips[way]):
                leaf_copy(way, index, sub).wait_send()
    for copy in mass_copies(*stages[2]):
        copy.wait_send()


def step(sizes, densities, scaling, weights):
    n, ngx, ngy = sizes
    _, rows, cols = densities.shape
    frame = cols + 2 * LANES
    size = rows // n
    steps = (n // 2 - SKIPS[0], (n - 1) // 2 - SKIPS[1])
    extra = [max(k, 1) for k in SKIPS]
    out = jax.ShapeDtypeStruct((rows, cols), jnp.float32)
    vmem = pl.BlockSpec(memory_space=pltpu.VMEM)
    hbm = pl.BlockSpec(memory_space=pl.ANY)
    dma = pltpu.SemaphoreType.DMA
    f32, bf16 = jnp.float32, jnp.bfloat16
    raw, ku, norm = pl.pallas_call(
        functools.partial(kernel, sizes, rows, cols),
        out_shape=(out, out, jax.ShapeDtypeStruct((1, 1), f32)),
        in_specs=[hbm, hbm, pl.BlockSpec(memory_space=pltpu.SMEM)],
        out_specs=(vmem, vmem, vmem),
        scratch_shapes=[
            pltpu.VMEM((2, rows, rows), bf16),
            pltpu.VMEM((2, 2, HALF, HALF), bf16),
            pltpu.VMEM((2, 2 * BLOCK, BLOCK), bf16),
            pltpu.VMEM((2, rows, cols + LANES), f32),
            pltpu.VMEM((rows, cols), f32),
            pltpu.VMEM((2, 2, HALF, cols + LANES), f32),
            pltpu.VMEM((2, 2, rows // 4, LANES), f32),
            pltpu.VMEM((2, 2, rows // 4, LANES), f32),
            pltpu.VMEM((2, 2, 2, HALF, LANES), f32),
            pltpu.VMEM((rows, frame), bf16),
            pltpu.VMEM((rows, frame), bf16),
            pltpu.VMEM((2, HALF, cols + LANES), f32),
            pltpu.VMEM((rows, cols), f32),
            *[pltpu.VMEM((k, size, cols), f32) for k in (*steps, *extra)],
            pltpu.VMEM((3, 8, LANES), f32),
            pltpu.VMEM((ngx, 8, LANES), f32),
            pltpu.VMEM((ngy, 8, LANES), f32),
            pltpu.VMEM((n, 8, LANES), f32),
            dma((2,)),
            dma((2, 6 + 2 * (cols // BLOCK))),
            dma((2, 6 + 2 * (cols // BLOCK))),
            *[dma((2, k, SUBS)) for k in (*steps, *extra)],
            *[dma((2, k, SUBS)) for k in (*steps, *extra)],
            dma((2, ngx)),
            dma((2, ngy)),
            dma((2, n)),
        ],
        compiler_params=pltpu.CompilerParams(
            collective_id=0, has_side_effects=True, vmem_limit_bytes=50 * 1024 * 1024
        ),
        name="sinkhorn",
    )(scaling, densities, weights)
    barycenter = raw * norm[0, 0]
    new_scaling = barycenter / ku
    return barycenter, new_scaling[None]


def solution(mesh):
    placed = (P("map", "gx", "gy"), P("map", "gx", "gy"), P("map"))
    sizes = (mesh.shape["map"], mesh.shape["gx"], mesh.shape["gy"])
    return jax.shard_map(
        functools.partial(step, sizes),
        mesh=mesh,
        in_specs=placed,
        out_specs=(P("gx", "gy"), P("map", "gx", "gy")),
        check_vma=False,
    )
```
